32 devices in a mesh: dom: 4 (over y, x), sep: 8 (over z, core).
Axes of the slice: x: 2, y: 2, z: 4, core: 2. Of those that a mesh axis runs over, the one named last changes fastest.
Arguments:
- rhs_leaf: bfloat16 [4, 4096, 1536], P('dom', 'sep'), may hold values from -6 to 6
- rhs_middle: bfloat16 [4, 4096, 768], P('dom', 'sep'), may hold values from -6 to 6
- rhs_top: bfloat16 [4, 4096, 384], P('dom', 'sep'), may hold values from -6 to 6
- update_leaf: bfloat16 [4, 4096, 256], P('dom', 'sep'), may hold values from -0.375 to 0.375
- couple_leaf: bfloat16 [4, 4096, 256], P('dom', 'sep'), may hold values from -0.09375 to 0.09375
- update_middle: bfloat16 [4, 4096, 256], P('dom', 'sep'), may hold values from -0.375 to 0.375, as said below
- couple_middle: bfloat16 [4, 4096, 256], P('dom', 'sep'), may hold values from -0.09375 to 0.09375, as said below
- pivot_leaf: float32 [4, 4096], P('dom', 'sep'), may hold values from 2.2 to 4
- pivot_middle: float32 [2, 4096], P(None, 'sep'), may hold values from 2.2 to 4
- pivot_top: float32 [1, 4096], P(None, 'sep'), may hold values from 2.2 to 4
- front_rows: int32 [4, 8], P('dom', 'sep'), may hold values from 128 to 512, as said below
- rank_leaf: int32 [4], P('dom'), may hold values from 64 to 256, as said below
- rank_middle: int32 [2], replicated, may hold values from 64 to 256, as said below
Outputs:
- top_values: float32 [4, 4096, 384], P('dom', 'sep')
The draws below stay inside these ranges and needn't reach their ends.
Inputs may be any that keep to these rules, and one draw needn't show every extreme that they name: `front_rows`: in every draw some front has all 512 rows of some row block live. `rank_leaf`: some leaf front has rank 256 in every draw. `rank_middle`: some middle front has rank 256 in every draw. `update_middle`: rows 2g and 2g+1 are equal; entries lie within plus or minus 6 / sqrt(256). `couple_middle`: rows 2g and 2g+1 are equal; entries lie within plus or minus 6 / sqrt(4096).
All inputs are finite; a program needn't handle non-finite values.
Results may differ from the reference program's by a relative error of at most 0.0018.
Values may be sent and summed in bfloat16 or wider, within the bound.
A program may use at most 64 MiB of HBM per device.

```python
import math
import jax
import jax.numpy as jnp
from jax import lax

ROWS = 512
SRC = 1536
RANK = 256
SEP = 4096
FRONTS = 4


def paired_factor(key, salt, fan_in):
    base_key = jax.random.fold_in(key, salt)
    base = jax.random.normal(base_key, (FRONTS // 2, SEP, RANK), jnp.float32)
    scaled = jnp.clip(base, -6.0, 6.0) * fan_in ** (-0.5)
    return jnp.repeat(scaled, 2, axis=0).astype(jnp.bfloat16)


def forced_ints(key, count, lowest, highest):
    first_key, second_key = jax.random.split(key)
    values = jax.random.randint(first_key, (count,), lowest, highest + 1, jnp.int32)
    target = jax.random.randint(second_key, (), 0, count, jnp.int32)
    return jnp.where(jnp.arange(count, dtype=jnp.int32) == target, jnp.int32(highest), values)


def draw_update_middle(key, part):
    return paired_factor(key, 11, RANK)


def draw_couple_middle(key, part):
    return paired_factor(key, 23, SEP)


def draw_front_rows(key, part):
    blocks = SEP // ROWS
    values = forced_ints(jax.random.fold_in(key, 31), FRONTS * blocks, max(1, ROWS // 4), ROWS)
    return values.reshape(FRONTS, blocks)


def draw_rank_leaf(key, part):
    return forced_ints(jax.random.fold_in(key, 41), FRONTS, max(1, RANK // 4), RANK)


def draw_rank_middle(key, part):
    return forced_ints(jax.random.fold_in(key, 53), FRONTS // 2, max(1, RANK // 4), RANK)


def block_levels(stream_key, shape, cuts, low, high):
    loudness = 1.0
    for axis_at, blocks in cuts:
        steps = jax.random.uniform(jax.random.fold_in(jax.random.fold_in(stream_key, 6), axis_at), (blocks,), jnp.float32, low / len(cuts), high / len(cuts))
        loudness = loudness * jnp.repeat(jnp.exp(steps), shape[axis_at] // blocks).reshape((-1,) + (1,) * (len(shape) - 1 - axis_at))
    return loudness


def centred(own_key, dims, width, most, shards=(), held_as=jnp.bfloat16):
    entries = jax.random.normal(own_key, dims, jnp.float32) * width
    if len(shards) > 0:
        entries = block_levels(own_key, dims, shards, -0.22, 0.18) * entries
    return jnp.clip(entries, min=-most, max=most).astype(held_as)


def setup_inputs(seed: int = 0) -> dict:
    splits = jax.random.split(jax.random.key(seed), 14)
    rhs_leaf = centred(splits[0], (FRONTS, SEP, SRC), 1.0, 6.0, ((0, 4), (1, 8)))
    rhs_middle = centred(splits[1], (FRONTS, SEP, SRC // 2), 1.0, 6.0, ((0, 4), (1, 8)))
    rhs_top = centred(splits[2], (FRONTS, SEP, SRC // 4), 1.0, 6.0, ((0, 4), (1, 8)))
    update_leaf = centred(splits[3], (FRONTS, SEP, RANK), RANK ** -0.5, 0.375, ((0, 4), (1, 8)))
    couple_leaf = centred(splits[4], (FRONTS, SEP, RANK), SEP ** -0.5, 0.09375, ((0, 4), (1, 8)))
    update_middle = draw_update_middle(jax.random.fold_in(splits[13], 71), 0)
    couple_middle = draw_couple_middle(jax.random.fold_in(splits[13], 71), 0)
    pivot_leaf = jnp.clip(jnp.exp(math.log(4.0) - 0.597837 * jax.random.uniform(splits[7], (FRONTS, SEP), jnp.float32) ** block_levels(splits[7], (FRONTS, SEP), ((0, 4), (1, 8)), -0.2, 0.2)), 2.2, 4.0)
    pivot_middle = jnp.clip(jnp.exp(math.log(4.0) - 0.597837 * jax.random.uniform(splits[8], (FRONTS // 2, SEP), jnp.float32) ** block_levels(splits[8], (FRONTS // 2, SEP), ((1, 8),), -0.2, 0.2)), 2.2, 4.0)
    pivot_top = jnp.clip(jnp.exp(math.log(4.0) - 0.597837 * jax.random.uniform(splits[9], (FRONTS // 4, SEP), jnp.float32) ** block_levels(splits[9], (FRONTS // 4, SEP), ((1, 8),), -0.2, 0.2)), 2.2, 4.0)
    front_rows = draw_front_rows(jax.random.fold_in(splits[13], 71), 0)
    rank_leaf = draw_rank_leaf(jax.random.fold_in(splits[13], 71), 0)
    rank_middle = draw_rank_middle(jax.random.fold_in(splits[13], 71), 0)
    return dict(rhs_leaf=rhs_leaf, rhs_middle=rhs_middle, rhs_top=rhs_top, update_leaf=update_leaf, couple_leaf=couple_leaf, update_middle=update_middle, couple_middle=couple_middle, pivot_leaf=pivot_leaf, pivot_middle=pivot_middle, pivot_top=pivot_top, front_rows=front_rows, rank_leaf=rank_leaf, rank_middle=rank_middle)


def sep_solve(right_side, pivots, row_mask):
    scaled = row_mask[:, None] * right_side / pivots[:, None]
    zero_row = jnp.zeros((1, right_side.shape[1]), scaled.dtype)
    beside = jnp.concatenate([zero_row, scaled[:-1]], 0) + jnp.concatenate([scaled[1:], zero_row], 0)
    return scaled + row_mask[:, None] * beside / pivots[:, None]


def coupling(factor, values, rank):
    partial_sum = lax.dot_general(factor, values, (((0,), (0,)), ((), ())), preferred_element_type=jnp.float32)
    rank_keep = (jnp.arange(RANK) < rank).astype(jnp.float32)
    return (partial_sum * rank_keep[:, None]).astype(jnp.bfloat16)


def reference(rhs_leaf, rhs_middle, rhs_top, update_leaf, couple_leaf, update_middle, couple_middle, pivot_leaf, pivot_middle, pivot_top, front_rows, rank_leaf, rank_middle):
    half_width = SRC // 2
    quarter = SRC // 4
    row_ids = jnp.arange(SEP)
    local_row = row_ids % ROWS
    row_block = row_ids // ROWS
    every_row = jnp.ones((SEP,), jnp.float32)

    def level_one(g):
        coefficient_list = []
        for child in (0, 1):
            leaf = 2 * g + child
            live = (local_row < front_rows[leaf][row_block]).astype(jnp.float32)
            values = sep_solve(rhs_leaf[leaf].astype(jnp.float32), pivot_leaf[leaf], live).astype(jnp.bfloat16)
            coefficient_list.append(coupling(couple_leaf[leaf], values, rank_leaf[leaf]))
        halves = []
        for side in (0, 1):
            running = rhs_middle[2 * g + side].astype(jnp.float32)
            for child in (0, 1):
                running = running - jnp.dot(update_leaf[2 * g + child], coefficient_list[child][:, side * half_width:(side + 1) * half_width], preferred_element_type=jnp.float32)
            halves.append(running)
        middle_rhs = jnp.concatenate(halves, 1)
        middle_values = sep_solve(middle_rhs, pivot_middle[g], every_row).astype(jnp.bfloat16)
        return coupling(couple_middle[2 * g], middle_values, rank_middle[g])

    middle_coef = lax.map(level_one, jnp.arange(FRONTS // 2, dtype=jnp.int32))

    def level_two(q):
        results = []
        for j in range(4):
            front = 4 * q + j
            column_start = (j % 2) * half_width + (j // 2) * quarter
            running = rhs_top[front].astype(jnp.float32)
            for child in (0, 1):
                middle = 2 * q + child
                running = running - jnp.dot(update_middle[2 * middle], middle_coef[middle][:, column_start:column_start + quarter], preferred_element_type=jnp.float32)
            results.append(sep_solve(running, pivot_top[q], every_row))
        return jnp.stack(results)

    top_values = lax.map(level_two, jnp.arange(FRONTS // 4, dtype=jnp.int32))
    return top_values.reshape(FRONTS, SEP, quarter)
```

```python
import functools

import jax
import jax.numpy as jnp
from jax import lax
from jax.experimental import pallas as pl
from jax.experimental.pallas import tpu as pltpu
from jax.sharding import PartitionSpec as P

MESH = pl.DeviceIdType.MESH
F32 = jnp.float32
BF16 = jnp.bfloat16
CW = 128
HOP = 5
LAND = 2
TILE = 16


def flipped(value, bit):
    return value + bit - 2 * bit * (lax.rem(value // bit, 2))


def spread(row, height):
    return jnp.broadcast_to(row, (height, row.shape[1])).T


def dot(a, b):
    return jnp.dot(a, b, preferred_element_type=F32)


def dot_rows(a, b):
    return lax.dot_general(a, b, (((0,), (0,)), ((), ())), preferred_element_type=F32)


def kernel(
    n_sep,
    rhs_leaf, rhs_middle, rhs_top, update_leaf, couple_leaf, update_middle, couple_middle,
    pivot_leaf, pivot_middle, pivot_top, front_rows_hbm, rank_leaf_hbm, rank_middle_hbm,
    out,
    front_rows, rank_leaf, rank_middle, pivot_v, pivot_edge,
    leaf_v, middle_v, top_v, top_edge, couple_l, couple_m, update_l, update_m,
    weights, turned_l, turned_high, turned_low,
    edges, edge_left, edge_right, pair_g_send, pair_g_recv, g_own, g_send, g_recv, g_twice,
    coef_l, m_own, m_send, m_recv, p_send, p_recv, own,
    right_send, right_recv, left_send, left_recv, coef_m,
    load_sem, edge_send_sem, edge_recv_sem, tile_send_sem, tile_recv_sem,
    factor_send_sem, factor_recv_sem, pair_send_sem, pair_recv_sem, g_send_sem, g_recv_sem,
    coef_send_sem, coef_recv_sem, p_send_sem, p_recv_sem,
    right_send_sem, right_recv_sem, left_send_sem, left_recv_sem,
    final_send_sem, final_recv_sem,
):
    front = lax.axis_index("dom")
    sep = lax.axis_index("sep")
    n_z = n_sep // 2
    z = sep // 2
    core = lax.rem(sep, 2)
    side = lax.rem(front, 2)
    group = lax.rem(front // 2, 2)
    across = flipped(front, 1)
    over = flipped(front, 2)
    beyond = flipped(across, 2)
    sibling = flipped(sep, 1)

    rows, width = leaf_v.shape
    half = width // 2
    quarter = width // 4
    rank = couple_l.shape[1]
    hr = rank // 2
    n_top = quarter // CW
    items = 2 * n_top

    def load(src, dst, slot):
        return pltpu.make_async_copy(src, dst, load_sem.at[slot])

    loads = [
        load(front_rows_hbm, front_rows, 0),
        load(rank_leaf_hbm, rank_leaf, 1),
        load(rank_middle_hbm, rank_middle, 2),
        load(pivot_middle.at[pl.ds(front // 2, 1)], pivot_v.at[1], 3),
        load(couple_middle.at[0], couple_m, 4),
        load(update_leaf.at[0], update_l, 5),
        load(pivot_leaf, pivot_v.at[0], 6),
        load(couple_leaf.at[0], couple_l, 7),
        load(pivot_top.at[pl.ds(front // 4, 1)], pivot_v.at[2], 8),
        load(update_middle.at[0], update_m.at[group, pl.ds(0, rows)], 9),
        load(rhs_top.at[0], top_v, 10),
        load(rhs_leaf.at[0], leaf_v, 11),
        load(rhs_middle.at[0], middle_v, 12),
    ]
    for one in loads:
        one.start()

    barrier = pltpu.get_barrier_semaphore()

    def greet(dom_at, sep_at):
        pl.semaphore_signal(barrier, inc=1, device_id=(dom_at, sep_at), device_id_type=MESH)

    for k in range(1, n_sep):
        greet(front, lax.rem(sep + k, n_sep))
    for dom_at in (across, over, beyond):
        greet(dom_at, sep)
    has_prev = (sep > 0).astype(jnp.int32)
    has_next = (sep < n_sep - 1).astype(jnp.int32)

    @pl.when(sep > 0)
    def _():
        greet(over, sep - 1)

    @pl.when(sep < n_sep - 1)
    def _():
        greet(over, sep + 1)

    def clear(way):
        pivot_edge[way] = jnp.ones(pivot_edge.shape[1:], F32)
        top_edge[way] = jnp.zeros(top_edge.shape[1:], BF16)
        for g in range(2):
            update_m[g, rows + way * TILE : rows + (way + 1) * TILE, :] = jnp.zeros(
                (TILE, rank), BF16
            )

    @pl.when(sep == 0)
    def _():
        clear(0)

    @pl.when(sep == n_sep - 1)
    def _():
        clear(1)

    @pl.when(z == 0)
    def _():
        right_recv[...] = jnp.zeros(right_recv.shape, BF16)

    @pl.when(z == n_z - 1)
    def _():
        left_recv[...] = jnp.zeros(left_recv.shape, BF16)

    row_at = lax.broadcasted_iota(jnp.int32, (rows, CW), 0)
    lane_at = lax.broadcasted_iota(jnp.int32, (rows, CW), 1)

    def shifted(scaled, before, after):
        up = jnp.where(row_at == 0, before, pltpu.roll(scaled, 1, 0))
        down = jnp.where(row_at == rows - 1, after, pltpu.roll(scaled, rows - 1, 0))
        return up + down

    def half_at(which):
        return pl.multiple_of(hr * which, hr)

    def weighed(couple, which, weight, rank_now):
        at = half_at(which)
        kept = jnp.where(lane_at + at < rank_now, couple[:, pl.ds(at, hr)].astype(F32), 0.0)
        scaled = kept * weight
        return scaled, scaled + weight * shifted(scaled, 0.0, 0.0)

    def note(column, which, scaled):
        at = half_at(which)
        for end, edge_row in ((0, rows - 1), (1, 0)):
            edges[sep, :, pl.ds((column + end) * rank + at, hr)] = scaled[edge_row : edge_row + 1]

    rank_leaf_now = None
    for one in loads[:5]:
        one.wait()
    rank_leaf_now = rank_leaf[0]
    rank_middle_now = rank_middle[front // 2]
    weights[1] = 1.0 / spread(pivot_v[1], CW)
    for part, which in ((1, 1 - core), (0, core)):
        scaled, full = weighed(couple_m, which, weights[1], rank_middle_now)
        note(0, which, scaled)
        turned = full.T
        high = turned.astype(BF16)
        turned_high[part * hr : (part + 1) * hr, :] = high
        turned_low[part * hr : (part + 1) * hr, :] = (turned - high.astype(F32)).astype(BF16)

    loads[5].wait()

    def by_middle(part, right):
        block = slice(part * hr, (part + 1) * hr)
        return dot(turned_high[block, :], right) + dot(turned_low[block, :], right)

    pair_g_send[...] = by_middle(1, update_l[...])

    pl.semaphore_wait(barrier, n_sep + 2 + has_prev + has_next)

    def to_device(src, dst, send_sem, recv_sem, dom_at, sep_at):
        return pltpu.make_async_remote_copy(
            src, dst, send_sem, recv_sem, device_id=(dom_at, sep_at), device_id_type=MESH
        )

    pair_g = to_device(
        pair_g_send, pair_g_recv, pair_send_sem.at[0], pair_recv_sem.at[0], front, sibling
    )
    pair_g.start()
    g_own[...] = by_middle(0, update_l[...])

    for end, edge_row in ((0, rows - 1), (1, 0)):
        block = pl.ds(rows - TILE if end == 0 else 0, TILE)
        pick = TILE - 1 if end == 0 else 0
        row = update_l[block, :].astype(F32)[pick : pick + 1]
        edges[sep, :, (2 + end) * rank : (3 + end) * rank] = (
            row * weights[1, block, :][pick : pick + 1, :1]
        )

    for one in loads[6:8]:
        one.wait()
    live = (row_at < front_rows[0, 0]).astype(F32)
    weights[0] = live * (1.0 / spread(pivot_v[0], CW))
    for which in range(2):
        scaled, full = weighed(couple_l, which, weights[0], rank_leaf_now)
        note(4, which, scaled)
        turned_l[which * hr : (which + 1) * hr, :] = full.astype(BF16).T

    def edge_copy(sep_at, source):
        return to_device(
            edges.at[source], edges.at[source], edge_send_sem.at[sep_at],
            edge_recv_sem.at[source], front, sep_at,
        )

    pair_g.wait_recv()
    summed = g_own[...] + pair_g_recv[...]
    g_own[...] = summed
    g_send[...] = summed.astype(BF16)

    def g_copy(z_at, source):
        return to_device(
            g_send, g_recv.at[source], g_send_sem.at[z_at], g_recv_sem.at[source],
            front, 2 * z_at + core,
        )

    for k in range(1, n_sep):
        edge_copy(lax.rem(sep + k, n_sep), sep).start()
    for k in range(1, n_z):
        g_copy(lax.rem(z + k, n_z), z).start()

    for one in loads[8:11]:
        one.wait()

    def tile_copies(way, sep_at):
        block = pl.ds(rows - TILE if way == 0 else 0, TILE)
        landing = pl.ds(rows + way * TILE, TILE)
        copies = [
            (pivot_v.at[2], pivot_edge.at[way], front),
            (top_v.at[block], top_edge.at[way], front),
            (update_m.at[group, block], update_m.at[group, landing], front),
            (update_m.at[group, block], update_m.at[group, landing], over),
        ]
        return [
            to_device(
                src, dst, tile_send_sem.at[way, n], tile_recv_sem.at[way, n], dom_at, sep_at
            )
            for n, (src, dst, dom_at) in enumerate(copies)
        ]

    to_next = tile_copies(0, sep + 1)
    to_prev = tile_copies(1, sep - 1)

    @pl.when(sep < n_sep - 1)
    def _():
        for copy in to_next:
            copy.start()

    @pl.when(sep > 0)
    def _():
        for copy in to_prev:
            copy.start()

    factor_copy = to_device(
        update_m.at[group, pl.ds(0, rows)], update_m.at[group, pl.ds(0, rows)],
        factor_send_sem.at[0], factor_recv_sem.at[0], over, sep,
    )
    factor_copy.start()
    weights[2] = 1.0 / spread(pivot_v[2], CW)

    for one in loads[11:]:
        one.wait()
    for k in range(1, n_sep):
        edge_copy(0, lax.rem(sep + k, n_sep)).wait_recv()

    sixteen = lax.broadcasted_iota(jnp.int32, (TILE, rank), 0)
    before_at = jnp.maximum(sep - 1, 0)
    after_at = jnp.minimum(sep + 1, n_sep - 1)

    def two_rows(height_at, first, second):
        return jnp.where(height_at == 0, first, jnp.where(height_at == 1, second, 0.0)).astype(BF16)

    def neighbours(column):
        before = edges[before_at, :, column * rank : (column + 1) * rank]
        after = edges[after_at, :, (column + 1) * rank : (column + 2) * rank]
        return two_rows(
            sixteen, jnp.where(sep > 0, before, 0.0), jnp.where(sep < n_sep - 1, after, 0.0)
        )

    def end_rows(right, which, columns):
        first = right[0:TILE, columns].astype(F32)[0:1] * weights[which, 0:TILE, :][0:1, :1]
        last = (
            right[rows - TILE : rows, columns].astype(F32)[TILE - 1 :]
            * weights[which, rows - TILE : rows, :][TILE - 1 :, :1]
        )
        return two_rows(
            lax.broadcasted_iota(jnp.int32, (TILE, first.shape[1]), 0), first, last
        )

    edge_left[...] = neighbours(4)

    def coef_copy(n):
        columns = pl.ds(n * quarter, quarter)
        return to_device(
            coef_l.at[pl.ds(0, rank), columns], coef_l.at[pl.ds(rank, rank), columns],
            coef_send_sem.at[n], coef_recv_sem.at[n], front, sibling,
        )

    for n in range(4):
        columns = slice(n * quarter, (n + 1) * quarter)
        coef_l[0:rank, columns] = (
            dot(turned_l[...], leaf_v[:, columns])
            + dot_rows(edge_left[...], end_rows(leaf_v, 0, columns))
        ).astype(BF16)
        coef_copy(n).start()

    edge_left[...] = neighbours(0)
    m_pair = to_device(m_send, m_recv, pair_send_sem.at[1], pair_recv_sem.at[1], front, sibling)
    for part, which, target in ((1, 1 - core, m_send), (0, core, m_own)):
        for n in range(2):
            columns = slice(n * quarter, (n + 1) * quarter)
            target[:, columns] = by_middle(part, middle_v[:, columns]) + dot_rows(
                edge_left[:, pl.ds(half_at(which), hr)], end_rows(middle_v, 1, columns)
            )
        if part == 1:
            m_pair.start()

    own_lanes = half_at(core)
    for b in range(n_sep):
        if b < n_sep - 1:
            left = (
                edges[b, :, pl.ds(own_lanes, hr)], edges[b + 1, :, pl.ds(rank + own_lanes, hr)],
            )
            right = (
                edges[b + 1, :, 3 * rank : 4 * rank], edges[b, :, 2 * rank : 3 * rank],
            )
        else:
            left = (jnp.zeros((1, hr), F32),) * 2
            right = (jnp.zeros((1, rank), F32),) * 2
        for n in range(2):
            edge_right[2 * b + n : 2 * b + n + 1, :rank] = right[n]
            edge_right[2 * b + n : 2 * b + n + 1, rank:] = left[n]
    total = g_own[...] + dot_rows(
        edge_right[:, rank:].astype(BF16), edge_right[:, :rank].astype(BF16)
    )
    m_pair.wait_recv()
    m_own[...] += m_recv[...]
    for n in range(4):
        coef_copy(n).wait_recv()
    g_own[...] = total
    for k in range(1, n_z):
        source = lax.rem(z + k, n_z)
        g_copy(0, source).wait_recv()
        g_own[...] += g_recv[source].astype(F32)
    negated = (-g_own[...]).astype(BF16)
    g_twice[:, :rank] = negated
    g_twice[:, rank:] = negated

    targets = (across, over, beyond)

    def p_copy(n, j):
        return to_device(
            p_send.at[n, j], p_recv.at[n, j], p_send_sem.at[n, j], p_recv_sem.at[n, j],
            targets[n], sep,
        )

    def piece(side_at, group_at, j):
        at = pl.multiple_of(side_at * half + group_at * quarter + j * CW, CW)
        return dot(g_twice[...], coef_l[:, pl.ds(at, CW)])

    def m_piece(group_at, j):
        return m_own[:, pl.ds(pl.multiple_of(group_at * quarter + j * CW, CW), CW)]

    for j in range(n_top):
        p_send[2, j] = piece(1 - side, 1 - group, j).astype(BF16)
        p_copy(2, j).start()
        p_send[1, j] = (piece(side, 1 - group, j) + m_piece(1 - group, j)).astype(BF16)
        p_copy(1, j).start()
        p_send[0, j] = piece(1 - side, group, j).astype(BF16)
        p_copy(0, j).start()
        own[2 * j] = piece(side, group, j) + m_piece(group, j)

    @pl.when(sep > 0)
    def _():
        for copy in to_next:
            copy.wait_recv()

    @pl.when(sep < n_sep - 1)
    def _():
        for copy in to_prev:
            copy.wait_recv()

    factor_copy.wait_recv()

    def right_copy(i):
        return to_device(
            right_send.at[i], right_recv.at[i], right_send_sem.at[i], right_recv_sem.at[i],
            front, sep + 2,
        )

    def left_copy(i):
        return to_device(
            left_send.at[i], left_recv.at[i], left_send_sem.at[i], left_recv_sem.at[i],
            front, sep - 2,
        )

    def final_copy(i):
        at = lax.rem(i, 2)
        place = coef_m.at[
            group + at - 2 * group * at, lax.div(i, 2), :, pl.ds(half_at(core), hr)
        ]
        return to_device(
            place, place, final_send_sem.at[i], final_recv_sem.at[i], front, sibling
        )

    def gather(i):
        j = lax.div(i, 2)

        @pl.when(lax.rem(i, 2) == 0)
        def _():
            p_copy(0, j).wait_recv()
            own[i] += p_recv[0, j].astype(F32)

        @pl.when(lax.rem(i, 2) == 1)
        def _():
            p_copy(1, j).wait_recv()
            p_copy(2, j).wait_recv()
            own[i] = p_recv[1, j].astype(F32) + p_recv[2, j].astype(F32)

    def prefix(i):
        @pl.when(z > 0)
        def _():
            right_copy(i).wait_recv()

        @pl.when(z < n_z - 1)
        def _():
            right_send[i] = (own[i] + right_recv[i].astype(F32)).astype(BF16)
            right_copy(i).start()

    def suffix(i):
        @pl.when(z < n_z - 1)
        def _():
            left_copy(i).wait_recv()

        @pl.when(z > 0)
        def _():
            left_send[i] = (own[i] + left_recv[i].astype(F32)).astype(BF16)
            left_copy(i).start()

    def final(i):
        total = own[i] + right_recv[i].astype(F32) + left_recv[i].astype(F32)
        high = total.astype(BF16)
        low = (total - high.astype(F32)).astype(BF16)
        at = lax.rem(i, 2)
        group_at = group + at - 2 * group * at
        coef_m[group_at, lax.div(i, 2), 0, pl.ds(half_at(core), hr)] = high
        coef_m[group_at, lax.div(i, 2), 1, pl.ds(half_at(core), hr)] = low
        final_copy(i).start()

    def top(j):
        final_copy(2 * j).wait_recv()
        final_copy(2 * j + 1).wait_recv()
        at = pl.multiple_of(j * CW, CW)
        taken = (
            dot(update_m[0], coef_m[0, j, 0]) + dot(update_m[1], coef_m[1, j, 0])
            + dot(update_m[0], coef_m[0, j, 1]) + dot(update_m[1], coef_m[1, j, 1])
        )
        before = (
            top_edge[0, :, pl.ds(at, CW)].astype(F32)[TILE - 1 :]
            - taken[rows + TILE - 1 : rows + TILE]
        ) / pivot_edge[0, :, rows - 1 :]
        after = (
            top_edge[1, :, pl.ds(at, CW)].astype(F32)[:1] - taken[rows + TILE : rows + TILE + 1]
        ) / pivot_edge[1, :, :1]
        scaled = (top_v[:, pl.ds(at, CW)].astype(F32) - taken[:rows]) * weights[2]
        out[0, :, pl.ds(at, CW)] = scaled + weights[2] * shifted(scaled, before, after)

    last = jnp.maximum(z, n_z - 1 - z) * HOP
    steps = (n_z - 1) * HOP + items + LAND

    def step(t, carry):
        def on(at, count, body):
            @pl.when(jnp.logical_and(at >= 0, at < count))
            def _():
                body(at)

        on(t, items, gather)
        on(t - z * HOP, items, prefix)
        on(t - (n_z - 1 - z) * HOP, items, suffix)
        on(t - last, items, final)
        done = t - last - 1 - LAND

        @pl.when(jnp.logical_and(done >= 0, jnp.logical_and(done < items, lax.rem(done, 2) == 0)))
        def _():
            top(lax.div(done, 2))

        return carry

    lax.fori_loop(0, steps, step, 0)

    pair_g.wait_send()
    m_pair.wait_send()
    factor_copy.wait_send()
    for k in range(1, n_sep):
        edge_copy(lax.rem(sep + k, n_sep), sep).wait_send()
    for k in range(1, n_z):
        g_copy(lax.rem(z + k, n_z), z).wait_send()
    for n in range(4):
        coef_copy(n).wait_send()
    for n in range(3):
        for j in range(n_top):
            p_copy(n, j).wait_send()

    @pl.when(sep < n_sep - 1)
    def _():
        for copy in to_next:
            copy.wait_send()

    @pl.when(sep > 0)
    def _():
        for copy in to_prev:
            copy.wait_send()

    def drain(i, carry):
        @pl.when(z < n_z - 1)
        def _():
            right_copy(i).wait_send()

        @pl.when(z > 0)
        def _():
            left_copy(i).wait_send()

        final_copy(i).wait_send()
        return carry

    lax.fori_loop(0, items, drain, 0)


def shards(*operands):
    n_sep = lax.axis_size("sep")
    rows, width = operands[0].shape[1:]
    rank = operands[3].shape[2]
    half, quarter = width // 2, width // 4
    hr = rank // 2
    n_top = quarter // CW
    items = 2 * n_top
    dma = pltpu.SemaphoreType.DMA
    hbm = pl.BlockSpec(memory_space=pltpu.HBM)
    vmem = pl.BlockSpec(memory_space=pltpu.VMEM)
    return pl.pallas_call(
        functools.partial(kernel, n_sep),
        out_shape=jax.ShapeDtypeStruct((1, rows, quarter), F32),
        in_specs=[hbm] * 13,
        out_specs=vmem,
        scratch_shapes=[
            pltpu.SMEM(operands[10].shape, jnp.int32),
            pltpu.SMEM(operands[11].shape, jnp.int32),
            pltpu.SMEM(operands[12].shape, jnp.int32),
            pltpu.VMEM((3, 1, rows), F32),
            pltpu.VMEM((2, 1, rows), F32),
            pltpu.VMEM((rows, width), BF16),
            pltpu.VMEM((rows, half), BF16),
            pltpu.VMEM((rows, quarter), BF16),
            pltpu.VMEM((2, TILE, quarter), BF16),
            pltpu.VMEM((rows, rank), BF16),
            pltpu.VMEM((rows, rank), BF16),
            pltpu.VMEM((rows, rank), BF16),
            pltpu.VMEM((2, rows + 2 * TILE, rank), BF16),
            pltpu.VMEM((3, rows, CW), F32),
            pltpu.VMEM((rank, rows), BF16),
            pltpu.VMEM((rank, rows), BF16),
            pltpu.VMEM((rank, rows), BF16),
            pltpu.VMEM((n_sep, 1, 6 * rank), F32),
            pltpu.VMEM((TILE, rank), BF16),
            pltpu.VMEM((2 * n_sep, rank + hr), F32),
            pltpu.VMEM((hr, rank), F32),
            pltpu.VMEM((hr, rank), F32),
            pltpu.VMEM((hr, rank), F32),
            pltpu.VMEM((hr, rank), BF16),
            pltpu.VMEM((n_sep // 2, hr, rank), BF16),
            pltpu.VMEM((hr, 2 * rank), BF16),
            pltpu.VMEM((2 * rank, width), BF16),
            pltpu.VMEM((hr, half), F32),
            pltpu.VMEM((hr, half), F32),
            pltpu.VMEM((hr, half), F32),
            pltpu.VMEM((3, n_top, hr, CW), BF16),
            pltpu.VMEM((3, n_top, hr, CW), BF16),
            pltpu.VMEM((items, hr, CW), F32),
            pltpu.VMEM((items, hr, CW), BF16),
            pltpu.VMEM((items, hr, CW), BF16),
            pltpu.VMEM((items, hr, CW), BF16),
            pltpu.VMEM((items, hr, CW), BF16),
            pltpu.VMEM((2, n_top, 2, rank, CW), BF16),
            dma((13,)),
            dma((n_sep,)),
            dma((n_sep,)),
            dma((2, 4)),
            dma((2, 4)),
            dma((1,)),
            dma((1,)),
            dma((2,)),
            dma((2,)),
            dma((n_sep // 2,)),
            dma((n_sep // 2,)),
            dma((4,)),
            dma((4,)),
            dma((3, n_top)),
            dma((3, n_top)),
            dma((items,)),
            dma((items,)),
            dma((items,)),
            dma((items,)),
            dma((items,)),
            dma((items,)),
        ],
        compiler_params=pltpu.CompilerParams(
            collective_id=0, has_side_effects=True, vmem_limit_bytes=67043328
        ),
    )(*operands)


def solution(mesh):
    return jax.shard_map(
        shards,
        mesh=mesh,
        in_specs=(
            P("dom", "sep", None),
            P("dom", "sep", None),
            P("dom", "sep", None),
            P("dom", "sep", None),
            P("dom", "sep", None),
            P("dom", "sep", None),
            P("dom", "sep", None),
            P("dom", "sep"),
            P(None, "sep"),
            P(None, "sep"),
            P("dom", "sep"),
            P("dom"),
            P(),
        ),
        out_specs=P("dom", "sep", None),
        check_vma=False,
    )
```

```python
import functools

import jax
import jax.numpy as jnp
from jax import lax
from jax.experimental import pallas as pl
from jax.experimental.pallas import tpu as pltpu
from jax.sharding import PartitionSpec as P

MESH = pl.DeviceIdType.MESH
F32 = jnp.float32
BF16 = jnp.bfloat16
CW = 128
PARTS = 2
HOP = 5 * PARTS
LAND = 2 * PARTS
TILE = 16


def flipped(value, bit):
    return value + bit - 2 * bit * (lax.rem(value // bit, 2))


def spread(row, height):
    return jnp.broadcast_to(row, (height, row.shape[1])).T


def dot(a, b):
    return jnp.dot(a, b, preferred_element_type=F32)


def dot_rows(a, b):
    return lax.dot_general(a, b, (((0,), (0,)), ((), ())), preferred_element_type=F32)


def kernel(
    n_sep,
    rhs_leaf, rhs_middle, rhs_top, update_leaf, couple_leaf, update_middle, couple_middle,
    pivot_leaf, pivot_middle, pivot_top, front_rows_hbm, rank_leaf_hbm, rank_middle_hbm,
    out,
    front_rows, rank_leaf, rank_middle, pivot_v, pivot_edge,
    leaf_v, middle_v, top_v, top_edge, couple_l, couple_m, update_l, update_m,
    weights, turned_l, turned_high, turned_low,
    edges, edge_left, edge_right, pair_g_send, pair_g_recv, g_own, g_send, g_recv, g_twice,
    coef_l, m_own, m_send, m_recv, p_send, p_recv, own,
    right_send, right_recv, left_send, left_recv, coef_m,
    load_sem, edge_send_sem, edge_recv_sem, tile_send_sem, tile_recv_sem,
    factor_send_sem, factor_recv_sem, pair_send_sem, pair_recv_sem, g_send_sem, g_recv_sem,
    coef_send_sem, coef_recv_sem, p_send_sem, p_recv_sem,
    right_send_sem, right_recv_sem, left_send_sem, left_recv_sem,
    final_send_sem, final_recv_sem,
):
    front = lax.axis_index("dom")
    sep = lax.axis_index("sep")
    n_z = n_sep // 2
    z = sep // 2
    core = lax.rem(sep, 2)
    side = lax.rem(front, 2)
    group = lax.rem(front // 2, 2)
    across = flipped(front, 1)
    over = flipped(front, 2)
    beyond = flipped(across, 2)
    sibling = flipped(sep, 1)

    rows, width = leaf_v.shape
    half = width // 2
    quarter = width // 4
    rank = couple_l.shape[1]
    hr = rank // 2
    n_top = quarter // CW
    hp = hr // PARTS
    pieces = 2 * n_top
    items = PARTS * pieces

    def load(src, dst, slot):
        return pltpu.make_async_copy(src, dst, load_sem.at[slot])

    loads = [
        load(front_rows_hbm, front_rows, 0),
        load(rank_leaf_hbm, rank_leaf, 1),
        load(rank_middle_hbm, rank_middle, 2),
        load(pivot_middle.at[pl.ds(front // 2, 1)], pivot_v.at[1], 3),
        load(couple_middle.at[0], couple_m, 4),
        load(update_leaf.at[0], update_l, 5),
        load(pivot_leaf, pivot_v.at[0], 6),
        load(couple_leaf.at[0], couple_l, 7),
        load(pivot_top.at[pl.ds(front // 4, 1)], pivot_v.at[2], 8),
        load(update_middle.at[0], update_m.at[group, pl.ds(0, rows)], 9),
        load(rhs_top.at[0], top_v, 10),
        load(rhs_leaf.at[0], leaf_v, 11),
        load(rhs_middle.at[0], middle_v, 12),
    ]
    for one in loads:
        one.start()

    barrier = pltpu.get_barrier_semaphore()

    def greet(dom_at, sep_at):
        pl.semaphore_signal(barrier, inc=1, device_id=(dom_at, sep_at), device_id_type=MESH)

    for k in range(1, n_sep):
        greet(front, lax.rem(sep + k, n_sep))
    for dom_at in (across, over, beyond):
        greet(dom_at, sep)
    has_prev = (sep > 0).astype(jnp.int32)
    has_next = (sep < n_sep - 1).astype(jnp.int32)

    @pl.when(sep > 0)
    def _():
        greet(over, sep - 1)

    @pl.when(sep < n_sep - 1)
    def _():
        greet(over, sep + 1)

    def clear(way):
        pivot_edge[way] = jnp.ones(pivot_edge.shape[1:], F32)
        top_edge[way] = jnp.zeros(top_edge.shape[1:], BF16)
        for g in range(2):
            update_m[g, rows + way * TILE : rows + (way + 1) * TILE, :] = jnp.zeros(
                (TILE, rank), BF16
            )

    @pl.when(sep == 0)
    def _():
        clear(0)

    @pl.when(sep == n_sep - 1)
    def _():
        clear(1)

    @pl.when(z == 0)
    def _():
        right_recv[...] = jnp.zeros(right_recv.shape, BF16)

    @pl.when(z == n_z - 1)
    def _():
        left_recv[...] = jnp.zeros(left_recv.shape, BF16)

    row_at = lax.broadcasted_iota(jnp.int32, (rows, CW), 0)
    lane_at = lax.broadcasted_iota(jnp.int32, (rows, CW), 1)

    def shifted(scaled, before, after):
        up = jnp.where(row_at == 0, before, pltpu.roll(scaled, 1, 0))
        down = jnp.where(row_at == rows - 1, after, pltpu.roll(scaled, rows - 1, 0))
        return up + down

    def half_at(which):
        return pl.multiple_of(hr * which, hr)

    def weighed(couple, which, weight, rank_now):
        at = half_at(which)
        kept = jnp.where(lane_at + at < rank_now, couple[:, pl.ds(at, hr)].astype(F32), 0.0)
        scaled = kept * weight
        return scaled, scaled + weight * shifted(scaled, 0.0, 0.0)

    def note(at, stride, scaled):
        for end, edge_row in ((0, rows - 1), (1, 0)):
            place = pl.multiple_of(at + end * stride, hr)
            edges[sep, :, pl.ds(place, hr)] = scaled[edge_row : edge_row + 1]

    rank_leaf_now = None
    for one in loads[:5]:
        one.wait()
    rank_leaf_now = rank_leaf[0]
    rank_middle_now = rank_middle[front // 2]
    weights[1] = 1.0 / spread(pivot_v[1], CW)
    for part, which in ((1, 1 - core), (0, core)):
        scaled, full = weighed(couple_m, which, weights[1], rank_middle_now)
        note(which * 6 * hr, hr, scaled)
        turned = full.T
        high = turned.astype(BF16)
        turned_high[part * hr : (part + 1) * hr, :] = high
        turned_low[part * hr : (part + 1) * hr, :] = (turned - high.astype(F32)).astype(BF16)

    loads[5].wait()

    def by_middle(part, right):
        block = slice(part * hr, (part + 1) * hr)
        return dot(turned_high[block, :], right) + dot(turned_low[block, :], right)

    pair_g_send[...] = by_middle(1, update_l[...])

    pl.semaphore_wait(barrier, n_sep + 2 + has_prev + has_next)

    def to_device(src, dst, send_sem, recv_sem, dom_at, sep_at):
        return pltpu.make_async_remote_copy(
            src, dst, send_sem, recv_sem, device_id=(dom_at, sep_at), device_id_type=MESH
        )

    pair_g = to_device(
        pair_g_send, pair_g_recv, pair_send_sem.at[0], pair_recv_sem.at[0], front, sibling
    )
    pair_g.start()
    g_own[...] = by_middle(0, update_l[...])

    for end, edge_row in ((0, rows - 1), (1, 0)):
        block = pl.ds(rows - TILE if end == 0 else 0, TILE)
        pick = TILE - 1 if end == 0 else 0
        row = update_l[block, :].astype(F32)[pick : pick + 1]
        edges[sep, :, (1 + end) * rank : (2 + end) * rank] = (
            row * weights[1, block, :][pick : pick + 1, :1]
        )

    for one in loads[6:8]:
        one.wait()
    live = (row_at < front_rows[0, 0]).astype(F32)
    weights[0] = live * (1.0 / spread(pivot_v[0], CW))
    for which in range(2):
        scaled, full = weighed(couple_l, which, weights[0], rank_leaf_now)
        note((8 + which) * hr, rank, scaled)
        turned_l[which * hr : (which + 1) * hr, :] = full.astype(BF16).T

    def edge_copy(k, sep_at, source, core_at):
        place = edges.at[source]
        if k not in (1, n_sep - 1):
            place = edges.at[source, :, pl.ds(pl.multiple_of(rank * core_at, rank), 6 * hr)]
        return to_device(
            place, place, edge_send_sem.at[sep_at], edge_recv_sem.at[source], front, sep_at
        )

    def edge_out(k):
        sep_at = lax.rem(sep + k, n_sep)
        return edge_copy(k, sep_at, sep, lax.rem(sep_at, 2))

    def edge_in(k):
        return edge_copy(n_sep - k, 0, lax.rem(sep + k, n_sep), core)

    near = (1, n_sep - 1)
    far = range(2, n_sep - 1)
    for k in near:
        edge_out(k).start()

    pair_g.wait_recv()
    summed = g_own[...] + pair_g_recv[...]
    g_own[...] = summed
    for part in range(PARTS):
        g_send[part] = summed[part * hp : (part + 1) * hp].astype(BF16)

    def g_copy(z_at, source, part):
        return to_device(
            g_send.at[part], g_recv.at[source, part], g_send_sem.at[z_at, part],
            g_recv_sem.at[source, part], front, 2 * z_at + core,
        )

    for part in range(PARTS):
        for k in range(1, n_z):
            g_copy(lax.rem(z + k, n_z), z, part).start()
        if part == 0:
            for k in far:
                edge_out(k).start()

    for one in loads[8:11]:
        one.wait()

    def tile_copies(way, sep_at):
        block = pl.ds(rows - TILE if way == 0 else 0, TILE)
        landing = pl.ds(rows + way * TILE, TILE)
        copies = [
            (pivot_v.at[2], pivot_edge.at[way], front),
            (top_v.at[block], top_edge.at[way], front),
            (update_m.at[group, block], update_m.at[group, landing], front),
            (update_m.at[group, block], update_m.at[group, landing], over),
        ]
        return [
            to_device(
                src, dst, tile_send_sem.at[way, n], tile_recv_sem.at[way, n], dom_at, sep_at
            )
            for n, (src, dst, dom_at) in enumerate(copies)
        ]

    to_next = tile_copies(0, sep + 1)
    to_prev = tile_copies(1, sep - 1)

    @pl.when(sep < n_sep - 1)
    def _():
        for copy in to_next:
            copy.start()

    @pl.when(sep > 0)
    def _():
        for copy in to_prev:
            copy.start()

    factor_copy = to_device(
        update_m.at[group, pl.ds(0, rows)], update_m.at[group, pl.ds(0, rows)],
        factor_send_sem.at[0], factor_recv_sem.at[0], over, sep,
    )
    factor_copy.start()
    weights[2] = 1.0 / spread(pivot_v[2], CW)

    for one in loads[11:]:
        one.wait()
    for k in near:
        edge_in(k).wait_recv()

    sixteen = lax.broadcasted_iota(jnp.int32, (TILE, hr), 0)
    before_at = jnp.maximum(sep - 1, 0)
    after_at = jnp.minimum(sep + 1, n_sep - 1)

    def two_rows(height_at, first, second):
        return jnp.where(height_at == 0, first, jnp.where(height_at == 1, second, 0.0)).astype(BF16)

    def neighbours(at, stride):
        before = edges[before_at, :, at : at + hr]
        after = edges[after_at, :, at + stride : at + stride + hr]
        return two_rows(
            sixteen, jnp.where(sep > 0, before, 0.0), jnp.where(sep < n_sep - 1, after, 0.0)
        )

    def end_rows(right, which, columns):
        first = right[0:TILE, columns].astype(F32)[0:1] * weights[which, 0:TILE, :][0:1, :1]
        last = (
            right[rows - TILE : rows, columns].astype(F32)[TILE - 1 :]
            * weights[which, rows - TILE : rows, :][TILE - 1 :, :1]
        )
        return two_rows(
            lax.broadcasted_iota(jnp.int32, (TILE, first.shape[1]), 0), first, last
        )

    edge_left[:, :hr] = neighbours(8 * hr, rank)
    edge_left[:, hr:] = neighbours(9 * hr, rank)

    def coef_copy(n):
        columns = pl.ds(n * quarter, quarter)
        return to_device(
            coef_l.at[pl.ds(0, rank), columns], coef_l.at[pl.ds(rank, rank), columns],
            coef_send_sem.at[n], coef_recv_sem.at[n], front, sibling,
        )

    for n in range(4):
        columns = slice(n * quarter, (n + 1) * quarter)
        coef_l[0:rank, columns] = (
            dot(turned_l[...], leaf_v[:, columns])
            + dot_rows(edge_left[...], end_rows(leaf_v, 0, columns))
        ).astype(BF16)
        coef_copy(n).start()

    edge_left[:, :hr] = neighbours(0, hr)
    edge_left[:, hr:] = neighbours(6 * hr, hr)
    m_pair = to_device(m_send, m_recv, pair_send_sem.at[1], pair_recv_sem.at[1], front, sibling)
    for part, which, target in ((1, 1 - core, m_send), (0, core, m_own)):
        for n in range(2):
            columns = slice(n * quarter, (n + 1) * quarter)
            target[:, columns] = by_middle(part, middle_v[:, columns]) + dot_rows(
                edge_left[:, pl.ds(half_at(which), hr)], end_rows(middle_v, 1, columns)
            )
        if part == 1:
            m_pair.start()

    for k in far:
        edge_in(k).wait_recv()
    own_lanes = pl.multiple_of(core * 6 * hr, hr)
    for b in range(n_sep):
        if b < n_sep - 1:
            left = (
                edges[b, :, pl.ds(own_lanes, hr)], edges[b + 1, :, pl.ds(own_lanes + hr, hr)],
            )
            right = (
                edges[b + 1, :, 2 * rank : 3 * rank], edges[b, :, rank : 2 * rank],
            )
        else:
            left = (jnp.zeros((1, hr), F32),) * 2
            right = (jnp.zeros((1, rank), F32),) * 2
        for n in range(2):
            edge_right[2 * b + n : 2 * b + n + 1, :rank] = right[n]
            edge_right[2 * b + n : 2 * b + n + 1, rank:] = left[n]
    total = g_own[...] + dot_rows(
        edge_right[:, rank:].astype(BF16), edge_right[:, :rank].astype(BF16)
    )
    m_pair.wait_recv()
    m_own[...] += m_recv[...]
    for n in range(4):
        coef_copy(n).wait_recv()
    g_own[...] = total
    targets = (across, over, beyond)

    def p_copy(n, part, j):
        return to_device(
            p_send.at[n, part, j], p_recv.at[n, part, j], p_send_sem.at[n, part * n_top + j],
            p_recv_sem.at[n, part * n_top + j], targets[n], sep,
        )

    for part in range(PARTS):
        block = slice(part * hp, (part + 1) * hp)
        for k in range(1, n_z):
            source = lax.rem(z + k, n_z)
            g_copy(0, source, part).wait_recv()
            g_own[block, :] += g_recv[source, part].astype(F32)
        negated = (-g_own[block, :]).astype(BF16)
        g_twice[block, :rank] = negated
        g_twice[block, rank:] = negated

        def piece(side_at, group_at, j):
            at = pl.multiple_of(side_at * half + group_at * quarter + j * CW, CW)
            return dot(g_twice[block, :], coef_l[:, pl.ds(at, CW)])

        def m_piece(group_at, j):
            return m_own[block, pl.ds(pl.multiple_of(group_at * quarter + j * CW, CW), CW)]

        for j in range(n_top):
            p_send[2, part, j] = piece(1 - side, 1 - group, j).astype(BF16)
            p_copy(2, part, j).start()
            p_send[1, part, j] = (
                piece(side, 1 - group, j) + m_piece(1 - group, j)
            ).astype(BF16)
            p_copy(1, part, j).start()
            p_send[0, part, j] = piece(1 - side, group, j).astype(BF16)
            p_copy(0, part, j).start()
            own[part * pieces + 2 * j] = piece(side, group, j) + m_piece(group, j)

    @pl.when(sep > 0)
    def _():
        for copy in to_next:
            copy.wait_recv()

    @pl.when(sep < n_sep - 1)
    def _():
        for copy in to_prev:
            copy.wait_recv()

    factor_copy.wait_recv()

    def right_copy(i):
        return to_device(
            right_send.at[i], right_recv.at[i], right_send_sem.at[i], right_recv_sem.at[i],
            front, sep + 2,
        )

    def left_copy(i):
        return to_device(
            left_send.at[i], left_recv.at[i], left_send_sem.at[i], left_recv_sem.at[i],
            front, sep - 2,
        )

    def place_of(i):
        at = lax.rem(i, 2)
        rest = lax.rem(i, pieces)
        start = pl.multiple_of(core * hr + lax.div(i, pieces) * hp, hp)
        return group + at - 2 * group * at, lax.div(rest, 2), pl.ds(start, hp)

    def final_copy(i):
        group_at, j, block = place_of(i)
        place = coef_m.at[group_at, j, :, block]
        return to_device(
            place, place, final_send_sem.at[i], final_recv_sem.at[i], front, sibling
        )

    def gather(i):
        part = lax.div(i, pieces)
        j = lax.div(lax.rem(i, pieces), 2)

        @pl.when(lax.rem(i, 2) == 0)
        def _():
            p_copy(0, part, j).wait_recv()
            own[i] += p_recv[0, part, j].astype(F32)

        @pl.when(lax.rem(i, 2) == 1)
        def _():
            p_copy(1, part, j).wait_recv()
            p_copy(2, part, j).wait_recv()
            own[i] = p_recv[1, part, j].astype(F32) + p_recv[2, part, j].astype(F32)

    def prefix(i):
        @pl.when(z > 0)
        def _():
            right_copy(i).wait_recv()

        @pl.when(z < n_z - 1)
        def _():
            right_send[i] = (own[i] + right_recv[i].astype(F32)).astype(BF16)
            right_copy(i).start()

    def suffix(i):
        @pl.when(z < n_z - 1)
        def _():
            left_copy(i).wait_recv()

        @pl.when(z > 0)
        def _():
            left_send[i] = (own[i] + left_recv[i].astype(F32)).astype(BF16)
            left_copy(i).start()

    def final(i):
        total = own[i] + right_recv[i].astype(F32) + left_recv[i].astype(F32)
        high = total.astype(BF16)
        low = (total - high.astype(F32)).astype(BF16)
        group_at, j, block = place_of(i)
        coef_m[group_at, j, 0, block] = high
        coef_m[group_at, j, 1, block] = low
        final_copy(i).start()

    def top(j):
        for part in range(PARTS):
            final_copy(part * pieces + 2 * j).wait_recv()
            final_copy(part * pieces + 2 * j + 1).wait_recv()
        at = pl.multiple_of(j * CW, CW)
        taken = (
            dot(update_m[0], coef_m[0, j, 0]) + dot(update_m[1], coef_m[1, j, 0])
            + dot(update_m[0], coef_m[0, j, 1]) + dot(update_m[1], coef_m[1, j, 1])
        )
        before = (
            top_edge[0, :, pl.ds(at, CW)].astype(F32)[TILE - 1 :]
            - taken[rows + TILE - 1 : rows + TILE]
        ) / pivot_edge[0, :, rows - 1 :]
        after = (
            top_edge[1, :, pl.ds(at, CW)].astype(F32)[:1] - taken[rows + TILE : rows + TILE + 1]
        ) / pivot_edge[1, :, :1]
        scaled = (top_v[:, pl.ds(at, CW)].astype(F32) - taken[:rows]) * weights[2]
        out[0, :, pl.ds(at, CW)] = scaled + weights[2] * shifted(scaled, before, after)

    last = jnp.maximum(z, n_z - 1 - z) * HOP
    steps = (n_z - 1) * HOP + items + LAND

    def step(t, carry):
        def on(at, count, body):
            @pl.when(jnp.logical_and(at >= 0, at < count))
            def _():
                body(at)

        on(t, items, gather)
        on(t - z * HOP, items, prefix)
        on(t - (n_z - 1 - z) * HOP, items, suffix)
        on(t - last, items, final)
        done = t - last - 1 - LAND - (items - pieces)

        @pl.when(jnp.logical_and(done >= 0, jnp.logical_and(done < pieces, lax.rem(done, 2) == 0)))
        def _():
            top(lax.div(done, 2))

        return carry

    lax.fori_loop(0, steps, step, 0)

    pair_g.wait_send()
    m_pair.wait_send()
    factor_copy.wait_send()
    for k in range(1, n_sep):
        edge_out(k).wait_send()
    for part in range(PARTS):
        for k in range(1, n_z):
            g_copy(lax.rem(z + k, n_z), z, part).wait_send()
    for n in range(4):
        coef_copy(n).wait_send()
    for n in range(3):
        for part in range(PARTS):
            for j in range(n_top):
                p_copy(n, part, j).wait_send()

    @pl.when(sep < n_sep - 1)
    def _():
        for copy in to_next:
            copy.wait_send()

    @pl.when(sep > 0)
    def _():
        for copy in to_prev:
            copy.wait_send()

    def drain(i, carry):
        @pl.when(z < n_z - 1)
        def _():
            right_copy(i).wait_send()

        @pl.when(z > 0)
        def _():
            left_copy(i).wait_send()

        final_copy(i).wait_send()
        return carry

    lax.fori_loop(0, items, drain, 0)


def shards(*operands):
    n_sep = lax.axis_size("sep")
    rows, width = operands[0].shape[1:]
    rank = operands[3].shape[2]
    half, quarter = width // 2, width // 4
    hr = rank // 2
    hp = hr // PARTS
    n_top = quarter // CW
    items = PARTS * 2 * n_top
    dma = pltpu.SemaphoreType.DMA
    hbm = pl.BlockSpec(memory_space=pltpu.HBM)
    vmem = pl.BlockSpec(memory_space=pltpu.VMEM)
    return pl.pallas_call(
        functools.partial(kernel, n_sep),
        out_shape=pltpu.VMEM((1, rows, quarter), F32),
        in_specs=[hbm] * 13,
        out_specs=vmem,
        scratch_shapes=[
            pltpu.SMEM(operands[10].shape, jnp.int32),
            pltpu.SMEM(operands[11].shape, jnp.int32),
            pltpu.SMEM(operands[12].shape, jnp.int32),
            pltpu.VMEM((3, 1, rows), F32),
            pltpu.VMEM((2, 1, rows), F32),
            pltpu.VMEM((rows, width), BF16),
            pltpu.VMEM((rows, half), BF16),
            pltpu.VMEM((rows, quarter), BF16),
            pltpu.VMEM((2, TILE, quarter), BF16),
            pltpu.VMEM((rows, rank), BF16),
            pltpu.VMEM((rows, rank), BF16),
            pltpu.VMEM((rows, rank), BF16),
            pltpu.VMEM((2, rows + 2 * TILE, rank), BF16),
            pltpu.VMEM((3, rows, CW), F32),
            pltpu.VMEM((rank, rows), BF16),
            pltpu.VMEM((rank, rows), BF16),
            pltpu.VMEM((rank, rows), BF16),
            pltpu.VMEM((n_sep, 1, 6 * rank), F32),
            pltpu.VMEM((TILE, rank), BF16),
            pltpu.VMEM((2 * n_sep, rank + hr), F32),
            pltpu.VMEM((hr, rank), F32),
            pltpu.VMEM((hr, rank), F32),
            pltpu.VMEM((hr, rank), F32),
            pltpu.VMEM((PARTS, hp, rank), BF16),
            pltpu.VMEM((n_sep // 2, PARTS, hp, rank), BF16),
            pltpu.VMEM((hr, 2 * rank), BF16),
            pltpu.VMEM((2 * rank, width), BF16),
            pltpu.VMEM((hr, half), F32),
            pltpu.VMEM((hr, half), F32),
            pltpu.VMEM((hr, half), F32),
            pltpu.VMEM((3, PARTS, n_top, hp, CW), BF16),
            pltpu.VMEM((3, PARTS, n_top, hp, CW), BF16),
            pltpu.VMEM((items, hp, CW), F32),
            pltpu.VMEM((items, hp, CW), BF16),
            pltpu.VMEM((items, hp, CW), BF16),
            pltpu.VMEM((items, hp, CW), BF16),
            pltpu.VMEM((items, hp, CW), BF16),
            pltpu.VMEM((2, n_top, 2, rank, CW), BF16),
            dma((13,)),
            dma((n_sep,)),
            dma((n_sep,)),
            dma((2, 4)),
            dma((2, 4)),
            dma((1,)),
            dma((1,)),
            dma((2,)),
            dma((2,)),
            dma((n_sep // 2, PARTS)),
            dma((n_sep // 2, PARTS)),
            dma((4,)),
            dma((4,)),
            dma((3, PARTS * n_top)),
            dma((3, PARTS * n_top)),
            dma((items,)),
            dma((items,)),
            dma((items,)),
            dma((items,)),
            dma((items,)),
            dma((items,)),
        ],
        compiler_params=pltpu.CompilerParams(
            collective_id=0, has_side_effects=True, vmem_limit_bytes=57543328
        ),
    )(*operands)


def solution(mesh):
    return jax.shard_map(
        shards,
        mesh=mesh,
        in_specs=(
            P("dom", "sep", None),
            P("dom", "sep", None),
            P("dom", "sep", None),
            P("dom", "sep", None),
            P("dom", "sep", None),
            P("dom", "sep", None),
            P("dom", "sep", None),
            P("dom", "sep"),
            P(None, "sep"),
            P(None, "sep"),
            P("dom", "sep"),
            P("dom"),
            P(),
        ),
        out_specs=P("dom", "sep", None),
        check_vma=False,
    )
```

```python
import functools

import jax
import jax.numpy as jnp
from jax import lax
from jax.experimental import pallas as pl
from jax.experimental.pallas import tpu as pltpu
from jax.sharding import PartitionSpec as P

MESH = pl.DeviceIdType.MESH
F32 = jnp.float32
BF16 = jnp.bfloat16
CW = 128
PARTS = 2
HOP = 12
LAND = 2 * PARTS
TILE = 16


def flipped(value, bit):
    return value + bit - 2 * bit * (lax.rem(value // bit, 2))


def spread(row, height):
    return jnp.broadcast_to(row, (height, row.shape[1])).T


def dot(a, b):
    return jnp.dot(a, b, preferred_element_type=F32)


def dot_rows(a, b):
    return lax.dot_general(a, b, (((0,), (0,)), ((), ())), preferred_element_type=F32)


def kernel(
    n_sep,
    rhs_leaf, rhs_middle, rhs_top, update_leaf, couple_leaf, update_middle, couple_middle,
    pivot_leaf, pivot_middle, pivot_top, front_rows_hbm, rank_leaf_hbm, rank_middle_hbm,
    out,
    front_rows, rank_leaf, rank_middle, pivot_v, pivot_edge,
    leaf_v, middle_v, top_v, top_edge, couple_l, couple_m, update_l, update_m,
    weights, turned_l, turned_high, turned_low,
    edges, edge_left, edge_right, pair_g_send, pair_g_recv, g_own, g_send, g_recv, g_twice, product,
    coef_l, m_own, m_send, m_recv, p_send, p_recv, own,
    right_send, right_recv, left_send, left_recv, coef_m,
    load_sem, edge_send_sem, edge_recv_sem, tile_send_sem, tile_recv_sem,
    factor_send_sem, factor_recv_sem, pair_send_sem, pair_recv_sem, g_send_sem, g_recv_sem,
    coef_send_sem, coef_recv_sem, p_send_sem, p_recv_sem,
    right_send_sem, right_recv_sem, left_send_sem, left_recv_sem,
    final_send_sem, final_recv_sem,
):
    front = lax.axis_index("dom")
    sep = lax.axis_index("sep")
    n_z = n_sep // 2
    z = sep // 2
    core = lax.rem(sep, 2)
    side = lax.rem(front, 2)
    group = lax.rem(front // 2, 2)
    across = flipped(front, 1)
    over = flipped(front, 2)
    beyond = flipped(across, 2)
    sibling = flipped(sep, 1)

    rows, width = leaf_v.shape
    half = width // 2
    quarter = width // 4
    rank = couple_l.shape[1]
    hr = rank // 2
    n_top = quarter // CW
    hp = hr // PARTS
    pieces = 2 * n_top
    items = PARTS * pieces

    def load(src, dst, slot):
        return pltpu.make_async_copy(src, dst, load_sem.at[slot])

    loads = [
        load(front_rows_hbm, front_rows, 0),
        load(rank_leaf_hbm, rank_leaf, 1),
        load(rank_middle_hbm, rank_middle, 2),
        load(pivot_middle.at[pl.ds(front // 2, 1)], pivot_v.at[1], 3),
        load(couple_middle.at[0], couple_m, 4),
        load(update_leaf.at[0], update_l, 5),
        load(pivot_leaf, pivot_v.at[0], 6),
        load(couple_leaf.at[0], couple_l, 7),
        load(pivot_top.at[pl.ds(front // 4, 1)], pivot_v.at[2], 8),
        load(update_middle.at[0], update_m.at[group, pl.ds(0, rows)], 9),
        load(rhs_top.at[0], top_v, 10),
        load(rhs_leaf.at[0], leaf_v, 11),
        load(rhs_middle.at[0], middle_v, 12),
    ]
    for one in loads:
        one.start()

    barrier = pltpu.get_barrier_semaphore()

    def greet(dom_at, sep_at):
        pl.semaphore_signal(barrier, inc=1, device_id=(dom_at, sep_at), device_id_type=MESH)

    for k in range(1, n_sep):
        greet(front, lax.rem(sep + k, n_sep))
    for dom_at in (across, over, beyond):
        greet(dom_at, sep)
    has_prev = (sep > 0).astype(jnp.int32)
    has_next = (sep < n_sep - 1).astype(jnp.int32)

    @pl.when(sep > 0)
    def _():
        greet(over, sep - 1)

    @pl.when(sep < n_sep - 1)
    def _():
        greet(over, sep + 1)

    def clear(way):
        pivot_edge[way] = jnp.ones(pivot_edge.shape[1:], F32)
        top_edge[way] = jnp.zeros(top_edge.shape[1:], BF16)
        for g in range(2):
            update_m[g, rows + way * TILE : rows + (way + 1) * TILE, :] = jnp.zeros(
                (TILE, rank), BF16
            )

    @pl.when(sep == 0)
    def _():
        clear(0)

    @pl.when(sep == n_sep - 1)
    def _():
        clear(1)

    @pl.when(z == 0)
    def _():
        right_recv[...] = jnp.zeros(right_recv.shape, BF16)

    @pl.when(z == n_z - 1)
    def _():
        left_recv[...] = jnp.zeros(left_recv.shape, BF16)

    row_at = lax.broadcasted_iota(jnp.int32, (rows, CW), 0)
    lane_at = lax.broadcasted_iota(jnp.int32, (rows, CW), 1)

    def shifted(scaled, before, after):
        up = jnp.where(row_at == 0, before, pltpu.roll(scaled, 1, 0))
        down = jnp.where(row_at == rows - 1, after, pltpu.roll(scaled, rows - 1, 0))
        return up + down

    def half_at(which):
        return pl.multiple_of(hr * which, hr)

    def weighed(couple, which, weight, rank_now):
        at = half_at(which)
        kept = jnp.where(lane_at + at < rank_now, couple[:, pl.ds(at, hr)].astype(F32), 0.0)
        scaled = kept * weight
        return scaled, scaled + weight * shifted(scaled, 0.0, 0.0)

    def note(at, stride, scaled):
        for end, edge_row in ((0, rows - 1), (1, 0)):
            place = pl.multiple_of(at + end * stride, hr)
            edges[sep, :, pl.ds(place, hr)] = scaled[edge_row : edge_row + 1]

    rank_leaf_now = None
    for one in loads[:5]:
        one.wait()
    rank_leaf_now = rank_leaf[0]
    rank_middle_now = rank_middle[front // 2]
    weights[1] = 1.0 / spread(pivot_v[1], CW)
    for part, which in ((1, 1 - core), (0, core)):
        scaled, full = weighed(couple_m, which, weights[1], rank_middle_now)
        note(which * 6 * hr, hr, scaled)
        turned = full.T
        high = turned.astype(BF16)
        turned_high[part * hr : (part + 1) * hr, :] = high
        turned_low[part * hr : (part + 1) * hr, :] = (turned - high.astype(F32)).astype(BF16)

    loads[5].wait()

    def by_middle(part, right):
        block = slice(part * hr, (part + 1) * hr)
        return dot(turned_high[block, :], right) + dot(turned_low[block, :], right)

    pair_g_send[...] = by_middle(1, update_l[...])

    pl.semaphore_wait(barrier, n_sep + 2 + has_prev + has_next)

    def to_device(src, dst, send_sem, recv_sem, dom_at, sep_at):
        return pltpu.make_async_remote_copy(
            src, dst, send_sem, recv_sem, device_id=(dom_at, sep_at), device_id_type=MESH
        )

    pair_g = to_device(
        pair_g_send, pair_g_recv, pair_send_sem.at[0], pair_recv_sem.at[0], front, sibling
    )
    pair_g.start()
    g_own[...] = by_middle(0, update_l[...])

    for end, edge_row in ((0, rows - 1), (1, 0)):
        block = pl.ds(rows - TILE if end == 0 else 0, TILE)
        pick = TILE - 1 if end == 0 else 0
        row = update_l[block, :].astype(F32)[pick : pick + 1]
        edges[sep, :, (1 + end) * rank : (2 + end) * rank] = (
            row * weights[1, block, :][pick : pick + 1, :1]
        )

    for one in loads[6:8]:
        one.wait()
    live = (row_at < front_rows[0, 0]).astype(F32)
    weights[0] = live * (1.0 / spread(pivot_v[0], CW))
    for which in range(2):
        scaled, full = weighed(couple_l, which, weights[0], rank_leaf_now)
        note((8 + which) * hr, rank, scaled)
        turned = full.T
        high = turned.astype(BF16)
        turned_l[0, which * hr : (which + 1) * hr, :] = high
        turned_l[1, which * hr : (which + 1) * hr, :] = (turned - high.astype(F32)).astype(BF16)

    def edge_copy(k, sep_at, source, core_at):
        place = edges.at[source]
        if k not in (1, n_sep - 1):
            place = edges.at[source, :, pl.ds(pl.multiple_of(rank * core_at, rank), 6 * hr)]
        return to_device(
            place, place, edge_send_sem.at[sep_at], edge_recv_sem.at[source], front, sep_at
        )

    def edge_out(k):
        sep_at = lax.rem(sep + k, n_sep)
        return edge_copy(k, sep_at, sep, lax.rem(sep_at, 2))

    def edge_in(k):
        return edge_copy(n_sep - k, 0, lax.rem(sep + k, n_sep), core)

    near = (1, n_sep - 1)
    far = range(2, n_sep - 1)
    for k in near:
        edge_out(k).start()

    pair_g.wait_recv()
    summed = g_own[...] + pair_g_recv[...]
    g_own[...] = summed
    for part in range(PARTS):
        g_send[part] = summed[part * hp : (part + 1) * hp].astype(BF16)

    def g_copy(z_at, source, part):
        return to_device(
            g_send.at[part], g_recv.at[source, part], g_send_sem.at[z_at, part],
            g_recv_sem.at[source, part], front, 2 * z_at + core,
        )

    for part in range(PARTS):
        for k in range(1, n_z):
            g_copy(lax.rem(z + k, n_z), z, part).start()
        if part == 0:
            for k in far:
                edge_out(k).start()

    for one in loads[8:11]:
        one.wait()

    def tile_copies(way, sep_at):
        block = pl.ds(rows - TILE if way == 0 else 0, TILE)
        landing = pl.ds(rows + way * TILE, TILE)
        copies = [
            (pivot_v.at[2], pivot_edge.at[way], front),
            (top_v.at[block], top_edge.at[way], front),
            (update_m.at[group, block], update_m.at[group, landing], front),
            (update_m.at[group, block], update_m.at[group, landing], over),
        ]
        return [
            to_device(
                src, dst, tile_send_sem.at[way, n], tile_recv_sem.at[way, n], dom_at, sep_at
            )
            for n, (src, dst, dom_at) in enumerate(copies)
        ]

    to_next = tile_copies(0, sep + 1)
    to_prev = tile_copies(1, sep - 1)

    @pl.when(sep < n_sep - 1)
    def _():
        for copy in to_next:
            copy.start()

    @pl.when(sep > 0)
    def _():
        for copy in to_prev:
            copy.start()

    factor_copy = to_device(
        update_m.at[group, pl.ds(0, rows)], update_m.at[group, pl.ds(0, rows)],
        factor_send_sem.at[0], factor_recv_sem.at[0], over, sep,
    )
    factor_copy.start()
    weights[2] = 1.0 / spread(pivot_v[2], CW)

    for one in loads[11:]:
        one.wait()
    for k in near:
        edge_in(k).wait_recv()

    sixteen = lax.broadcasted_iota(jnp.int32, (TILE, hr), 0)
    before_at = jnp.maximum(sep - 1, 0)
    after_at = jnp.minimum(sep + 1, n_sep - 1)

    def two_rows(height_at, first, second):
        return jnp.where(height_at == 0, first, jnp.where(height_at == 1, second, 0.0)).astype(BF16)

    def neighbours(at, stride):
        before = edges[before_at, :, at : at + hr]
        after = edges[after_at, :, at + stride : at + stride + hr]
        return two_rows(
            sixteen, jnp.where(sep > 0, before, 0.0), jnp.where(sep < n_sep - 1, after, 0.0)
        )

    def end_rows(right, which, columns):
        first = right[0:TILE, columns].astype(F32)[0:1] * weights[which, 0:TILE, :][0:1, :1]
        last = (
            right[rows - TILE : rows, columns].astype(F32)[TILE - 1 :]
            * weights[which, rows - TILE : rows, :][TILE - 1 :, :1]
        )
        return two_rows(
            lax.broadcasted_iota(jnp.int32, (TILE, first.shape[1]), 0), first, last
        )

    edge_left[:, :hr] = neighbours(8 * hr, rank)
    edge_left[:, hr:] = neighbours(9 * hr, rank)

    def coef_copy(n):
        columns = pl.ds(n * quarter, quarter)
        return to_device(
            coef_l.at[pl.ds(0, rank), columns], coef_l.at[pl.ds(rank, rank), columns],
            coef_send_sem.at[n], coef_recv_sem.at[n], front, sibling,
        )

    for n in range(4):
        columns = slice(n * quarter, (n + 1) * quarter)
        coef_l[0:rank, columns] = (
            dot(turned_l[0], leaf_v[:, columns]) + dot(turned_l[1], leaf_v[:, columns])
            + dot_rows(edge_left[...], end_rows(leaf_v, 0, columns))
        ).astype(BF16)
        coef_copy(n).start()

    edge_left[:, :hr] = neighbours(0, hr)
    edge_left[:, hr:] = neighbours(6 * hr, hr)
    m_pair = to_device(m_send, m_recv, pair_send_sem.at[1], pair_recv_sem.at[1], front, sibling)
    for part, which, target in ((1, 1 - core, m_send), (0, core, m_own)):
        for n in range(2):
            columns = slice(n * quarter, (n + 1) * quarter)
            target[:, columns] = by_middle(part, middle_v[:, columns]) + dot_rows(
                edge_left[:, pl.ds(half_at(which), hr)], end_rows(middle_v, 1, columns)
            )
        if part == 1:
            m_pair.start()

    for k in far:
        edge_in(k).wait_recv()
    own_lanes = pl.multiple_of(core * 6 * hr, hr)
    for b in range(n_sep):
        if b < n_sep - 1:
            left = (
                edges[b, :, pl.ds(own_lanes, hr)], edges[b + 1, :, pl.ds(own_lanes + hr, hr)],
            )
            right = (
                edges[b + 1, :, 2 * rank : 3 * rank], edges[b, :, rank : 2 * rank],
            )
        else:
            left = (jnp.zeros((1, hr), F32),) * 2
            right = (jnp.zeros((1, rank), F32),) * 2
        for n in range(2):
            edge_right[2 * b + n : 2 * b + n + 1, :rank] = right[n]
            edge_right[2 * b + n : 2 * b + n + 1, rank:] = left[n]
    total = g_own[...] + dot_rows(
        edge_right[:, rank:].astype(BF16), edge_right[:, :rank].astype(BF16)
    )
    m_pair.wait_recv()
    m_own[...] += m_recv[...]
    for n in range(4):
        coef_copy(n).wait_recv()
    g_own[...] = total
    targets = (across, over, beyond)

    def p_copy(n, part, j):
        return to_device(
            p_send.at[n, part, j], p_recv.at[n, part, j], p_send_sem.at[n, part * n_top + j],
            p_recv_sem.at[n, part * n_top + j], targets[n], sep,
        )

    for part in range(PARTS):
        block = slice(part * hp, (part + 1) * hp)
        for k in range(1, n_z):
            source = lax.rem(z + k, n_z)
            g_copy(0, source, part).wait_recv()
            g_own[block, :] += g_recv[source, part].astype(F32)
        negated = -g_own[block, :]
        high = negated.astype(BF16)
        low = (negated - high.astype(F32)).astype(BF16)
        for n in range(2):
            lanes = slice(n * rank, (n + 1) * rank)
            g_twice[part, :hp, lanes] = high
            g_twice[part, hp:, lanes] = low

        def multiply(side_at, slot):
            at = pl.multiple_of(side_at * half, half)
            both = dot(g_twice[part], coef_l[:, pl.ds(at, half)])
            product[slot] = both[:hp] + both[hp:]

        def piece(slot, group_at, j):
            at = pl.multiple_of(group_at * quarter + j * CW, CW)
            return product[slot, :, pl.ds(at, CW)]

        multiply(1 - side, 0)
        for j in range(n_top):
            for n, group_at in ((2, 1 - group), (0, group)):
                p_send[n, part, j] = piece(0, group_at, j).astype(BF16)
                p_copy(n, part, j).start()
        multiply(side, 1)
        product[1] += m_own[block, :]
        for j in range(n_top):
            p_send[1, part, j] = piece(1, 1 - group, j).astype(BF16)
            p_copy(1, part, j).start()
            own[part * pieces + 2 * j] = piece(1, group, j)

    @pl.when(sep > 0)
    def _():
        for copy in to_next:
            copy.wait_recv()

    @pl.when(sep < n_sep - 1)
    def _():
        for copy in to_prev:
            copy.wait_recv()

    factor_copy.wait_recv()

    def right_copy(i):
        return to_device(
            right_send.at[i], right_recv.at[i], right_send_sem.at[i], right_recv_sem.at[i],
            front, sep + 2,
        )

    def left_copy(i):
        return to_device(
            left_send.at[i], left_recv.at[i], left_send_sem.at[i], left_recv_sem.at[i],
            front, sep - 2,
        )

    def place_of(i):
        at = lax.rem(i, 2)
        rest = lax.rem(i, pieces)
        start = pl.multiple_of(core * hr + lax.div(i, pieces) * hp, hp)
        return group + at - 2 * group * at, lax.div(rest, 2), pl.ds(start, hp)

    def final_copy(i):
        group_at, j, block = place_of(i)
        place = coef_m.at[group_at, j, block]
        return to_device(
            place, place, final_send_sem.at[i], final_recv_sem.at[i], front, sibling
        )

    def gather(i):
        part = lax.div(i, pieces)
        j = lax.div(lax.rem(i, pieces), 2)

        @pl.when(lax.rem(i, 2) == 0)
        def _():
            p_copy(0, part, j).wait_recv()
            own[i] += p_recv[0, part, j].astype(F32)

        @pl.when(lax.rem(i, 2) == 1)
        def _():
            p_copy(1, part, j).wait_recv()
            p_copy(2, part, j).wait_recv()
            own[i] = p_recv[1, part, j].astype(F32) + p_recv[2, part, j].astype(F32)

    def prefix(i):
        @pl.when(z > 0)
        def _():
            right_copy(i).wait_recv()

        @pl.when(z < n_z - 1)
        def _():
            right_send[i] = (own[i] + right_recv[i].astype(F32)).astype(BF16)
            right_copy(i).start()

    def suffix(i):
        @pl.when(z < n_z - 1)
        def _():
            left_copy(i).wait_recv()

        @pl.when(z > 0)
        def _():
            left_send[i] = (own[i] + left_recv[i].astype(F32)).astype(BF16)
            left_copy(i).start()

    def final(i):
        total = own[i] + right_recv[i].astype(F32) + left_recv[i].astype(F32)
        high = total.astype(BF16)
        low = (total - high.astype(F32)).astype(BF16)
        group_at, j, block = place_of(i)
        coef_m[group_at, j, block, :CW] = high
        coef_m[group_at, j, block, CW:] = low
        final_copy(i).start()

    def top(j):
        for part in range(PARTS):
            final_copy(part * pieces + 2 * j).wait_recv()
            final_copy(part * pieces + 2 * j + 1).wait_recv()
        at = pl.multiple_of(j * CW, CW)
        both = dot(update_m[0], coef_m[0, j]) + dot(update_m[1], coef_m[1, j])
        taken = both[:, :CW] + both[:, CW:]
        before = (
            top_edge[0, :, pl.ds(at, CW)].astype(F32)[TILE - 1 :]
            - taken[rows + TILE - 1 : rows + TILE]
        ) / pivot_edge[0, :, rows - 1 :]
        after = (
            top_edge[1, :, pl.ds(at, CW)].astype(F32)[:1] - taken[rows + TILE : rows + TILE + 1]
        ) / pivot_edge[1, :, :1]
        scaled = (top_v[:, pl.ds(at, CW)].astype(F32) - taken[:rows]) * weights[2]
        out[0, :, pl.ds(at, CW)] = scaled + weights[2] * shifted(scaled, before, after)

    last = jnp.maximum(z, n_z - 1 - z) * HOP
    steps = (n_z - 1) * HOP + items + LAND

    def step(t, carry):
        def on(at, count, body):
            @pl.when(jnp.logical_and(at >= 0, at < count))
            def _():
                body(at)

        on(t, items, gather)
        on(t - z * HOP, items, prefix)
        on(t - (n_z - 1 - z) * HOP, items, suffix)
        on(t - last, items, final)
        done = t - last - 1 - LAND - (items - pieces)

        @pl.when(jnp.logical_and(done >= 0, jnp.logical_and(done < pieces, lax.rem(done, 2) == 0)))
        def _():
            top(lax.div(done, 2))

        return carry

    lax.fori_loop(0, steps, step, 0)

    pair_g.wait_send()
    m_pair.wait_send()
    factor_copy.wait_send()
    for k in range(1, n_sep):
        edge_out(k).wait_send()
    for part in range(PARTS):
        for k in range(1, n_z):
            g_copy(lax.rem(z + k, n_z), z, part).wait_send()
    for n in range(4):
        coef_copy(n).wait_send()
    for n in range(3):
        for part in range(PARTS):
            for j in range(n_top):
                p_copy(n, part, j).wait_send()

    @pl.when(sep < n_sep - 1)
    def _():
        for copy in to_next:
            copy.wait_send()

    @pl.when(sep > 0)
    def _():
        for copy in to_prev:
            copy.wait_send()

    def drain(i, carry):
        @pl.when(z < n_z - 1)
        def _():
            right_copy(i).wait_send()

        @pl.when(z > 0)
        def _():
            left_copy(i).wait_send()

        final_copy(i).wait_send()
        return carry

    lax.fori_loop(0, items, drain, 0)


def shards(*operands):
    n_sep = lax.axis_size("sep")
    rows, width = operands[0].shape[1:]
    rank = operands[3].shape[2]
    half, quarter = width // 2, width // 4
    hr = rank // 2
    hp = hr // PARTS
    n_top = quarter // CW
    items = PARTS * 2 * n_top
    dma = pltpu.SemaphoreType.DMA
    hbm = pl.BlockSpec(memory_space=pltpu.HBM)
    vmem = pl.BlockSpec(memory_space=pltpu.VMEM)
    return pl.pallas_call(
        functools.partial(kernel, n_sep),
        out_shape=pltpu.VMEM((1, rows, quarter), F32),
        in_specs=[hbm] * 13,
        out_specs=vmem,
        scratch_shapes=[
            pltpu.SMEM(operands[10].shape, jnp.int32),
            pltpu.SMEM(operands[11].shape, jnp.int32),
            pltpu.SMEM(operands[12].shape, jnp.int32),
            pltpu.VMEM((3, 1, rows), F32),
            pltpu.VMEM((2, 1, rows), F32),
            pltpu.VMEM((rows, width), BF16),
            pltpu.VMEM((rows, half), BF16),
            pltpu.VMEM((rows, quarter), BF16),
            pltpu.VMEM((2, TILE, quarter), BF16),
            pltpu.VMEM((rows, rank), BF16),
            pltpu.VMEM((rows, rank), BF16),
            pltpu.VMEM((rows, rank), BF16),
            pltpu.VMEM((2, rows + 2 * TILE, rank), BF16),
            pltpu.VMEM((3, rows, CW), F32),
            pltpu.VMEM((2, rank, rows), BF16),
            pltpu.VMEM((rank, rows), BF16),
            pltpu.VMEM((rank, rows), BF16),
            pltpu.VMEM((n_sep, 1, 6 * rank), F32),
            pltpu.VMEM((TILE, rank), BF16),
            pltpu.VMEM((2 * n_sep, rank + hr), F32),
            pltpu.VMEM((hr, rank), F32),
            pltpu.VMEM((hr, rank), F32),
            pltpu.VMEM((hr, rank), F32),
            pltpu.VMEM((PARTS, hp, rank), BF16),
            pltpu.VMEM((n_sep // 2, PARTS, hp, rank), BF16),
            pltpu.VMEM((PARTS, 2 * hp, 2 * rank), BF16),
            pltpu.VMEM((2, hp, half), F32),
            pltpu.VMEM((2 * rank, width), BF16),
            pltpu.VMEM((hr, half), F32),
            pltpu.VMEM((hr, half), F32),
            pltpu.VMEM((hr, half), F32),
            pltpu.VMEM((3, PARTS, n_top, hp, CW), BF16),
            pltpu.VMEM((3, PARTS, n_top, hp, CW), BF16),
            pltpu.VMEM((items, hp, CW), F32),
            pltpu.VMEM((items, hp, CW), BF16),
            pltpu.VMEM((items, hp, CW), BF16),
            pltpu.VMEM((items, hp, CW), BF16),
            pltpu.VMEM((items, hp, CW), BF16),
            pltpu.VMEM((2, n_top, rank, 2 * CW), BF16),
            dma((13,)),
            dma((n_sep,)),
            dma((n_sep,)),
            dma((2, 4)),
            dma((2, 4)),
            dma((1,)),
            dma((1,)),
            dma((2,)),
            dma((2,)),
            dma((n_sep // 2, PARTS)),
            dma((n_sep // 2, PARTS)),
            dma((4,)),
            dma((4,)),
            dma((3, PARTS * n_top)),
            dma((3, PARTS * n_top)),
            dma((items,)),
            dma((items,)),
            dma((items,)),
            dma((items,)),
            dma((items,)),
            dma((items,)),
        ],
        compiler_params=pltpu.CompilerParams(
            collective_id=0, has_side_effects=True, vmem_limit_bytes=57543328
        ),
    )(*operands)


def solution(mesh):
    return jax.shard_map(
        shards,
        mesh=mesh,
        in_specs=(
            P("dom", "sep", None),
            P("dom", "sep", None),
            P("dom", "sep", None),
            P("dom", "sep", None),
            P("dom", "sep", None),
            P("dom", "sep", None),
            P("dom", "sep", None),
            P("dom", "sep"),
            P(None, "sep"),
            P(None, "sep"),
            P("dom", "sep"),
            P("dom"),
            P(),
        ),
        out_specs=P("dom", "sep", None),
        check_vma=False,
    )
```

```python
import functools

import jax
import jax.numpy as jnp
from jax import lax
from jax.experimental import pallas as pl
from jax.experimental.pallas import tpu as pltpu
from jax.sharding import PartitionSpec as P

MESH = pl.DeviceIdType.MESH
F32 = jnp.float32
BF16 = jnp.bfloat16
CW = 128
PARTS = 2
HOP = 12
LAND = 2 * PARTS
TILE = 16


def flipped(value, bit):
    return value + bit - 2 * bit * (lax.rem(value // bit, 2))


def spread(row, height):
    return jnp.broadcast_to(row, (height, row.shape[1])).T


def dot(a, b):
    return jnp.dot(a, b, preferred_element_type=F32)


def dot_rows(a, b):
    return lax.dot_general(a, b, (((0,), (0,)), ((), ())), preferred_element_type=F32)


def kernel(
    n_sep,
    rhs_leaf, rhs_middle, rhs_top, update_leaf, couple_leaf, update_middle, couple_middle,
    pivot_leaf, pivot_middle, pivot_top, front_rows_hbm, rank_leaf_hbm, rank_middle_hbm,
    out,
    front_rows, rank_leaf, rank_middle, pivot_v, pivot_edge,
    leaf_v, middle_v, top_v, top_edge, couple_l, couple_m, update_l, update_m,
    weights, turned_l, turned_high, turned_low,
    edges, edge_left, edge_right, pair_g_send, pair_g_recv, g_own, g_send, g_recv, g_twice, product,
    coef_l, m_own, m_send, m_recv, p_send, p_recv, own,
    right_send, right_recv, left_send, left_recv, coef_m,
    load_sem, edge_send_sem, edge_recv_sem, tile_send_sem, tile_recv_sem,
    factor_send_sem, factor_recv_sem, pair_send_sem, pair_recv_sem, g_send_sem, g_recv_sem,
    coef_send_sem, coef_recv_sem, p_send_sem, p_recv_sem,
    right_send_sem, right_recv_sem, left_send_sem, left_recv_sem,
    final_send_sem, final_recv_sem,
):
    front = lax.axis_index("dom")
    sep = lax.axis_index("sep")
    n_z = n_sep // 2
    z = sep // 2
    core = lax.rem(sep, 2)
    side = lax.rem(front, 2)
    group = lax.rem(front // 2, 2)
    across = flipped(front, 1)
    over = flipped(front, 2)
    beyond = flipped(across, 2)
    sibling = flipped(sep, 1)

    rows, width = leaf_v.shape
    half = width // 2
    quarter = width // 4
    rank = couple_l.shape[1]
    hr = rank // 2
    n_top = quarter // CW
    hp = hr // PARTS
    pieces = 2 * n_top
    items = PARTS * pieces

    def load(src, dst, slot):
        return pltpu.make_async_copy(src, dst, load_sem.at[slot])

    loads = [
        load(front_rows_hbm, front_rows, 0),
        load(rank_leaf_hbm, rank_leaf, 1),
        load(rank_middle_hbm, rank_middle, 2),
        load(pivot_middle.at[pl.ds(front // 2, 1)], pivot_v.at[1], 3),
        load(couple_middle.at[0], couple_m, 4),
        load(update_leaf.at[0], update_l, 5),
        load(pivot_leaf, pivot_v.at[0], 6),
        load(couple_leaf.at[0], couple_l, 7),
        load(pivot_top.at[pl.ds(front // 4, 1)], pivot_v.at[2], 8),
        load(update_middle.at[0], update_m.at[group, pl.ds(0, rows)], 9),
        load(rhs_top.at[0], top_v, 10),
        load(rhs_leaf.at[0], leaf_v, 11),
        load(rhs_middle.at[0], middle_v, 12),
    ]
    for one in loads:
        one.start()

    barrier = pltpu.get_barrier_semaphore()

    def greet(dom_at, sep_at):
        pl.semaphore_signal(barrier, inc=1, device_id=(dom_at, sep_at), device_id_type=MESH)

    for k in range(1, n_sep):
        greet(front, lax.rem(sep + k, n_sep))
    for dom_at in (across, over, beyond):
        greet(dom_at, sep)
    has_prev = (sep > 0).astype(jnp.int32)
    has_next = (sep < n_sep - 1).astype(jnp.int32)

    @pl.when(sep > 0)
    def _():
        greet(over, sep - 1)

    @pl.when(sep < n_sep - 1)
    def _():
        greet(over, sep + 1)

    def clear(way):
        pivot_edge[way] = jnp.ones(pivot_edge.shape[1:], F32)
        top_edge[way] = jnp.zeros(top_edge.shape[1:], BF16)
        for g in range(2):
            update_m[g, rows + way * TILE : rows + (way + 1) * TILE, :] = jnp.zeros(
                (TILE, rank), BF16
            )

    @pl.when(sep == 0)
    def _():
        clear(0)

    @pl.when(sep == n_sep - 1)
    def _():
        clear(1)

    @pl.when(z == 0)
    def _():
        right_recv[...] = jnp.zeros(right_recv.shape, BF16)

    @pl.when(z == n_z - 1)
    def _():
        left_recv[...] = jnp.zeros(left_recv.shape, BF16)

    row_at = lax.broadcasted_iota(jnp.int32, (rows, CW), 0)
    lane_at = lax.broadcasted_iota(jnp.int32, (rows, CW), 1)

    def shifted(scaled, before, after):
        up = jnp.where(row_at == 0, before, pltpu.roll(scaled, 1, 0))
        down = jnp.where(row_at == rows - 1, after, pltpu.roll(scaled, rows - 1, 0))
        return up + down

    def half_at(which):
        return pl.multiple_of(hr * which, hr)

    def weighed(couple, which, weight, rank_now):
        at = half_at(which)
        kept = jnp.where(lane_at + at < rank_now, couple[:, pl.ds(at, hr)].astype(F32), 0.0)
        scaled = kept * weight
        return scaled, scaled + weight * shifted(scaled, 0.0, 0.0)

    def note(at, stride, scaled):
        for end, edge_row in ((0, rows - 1), (1, 0)):
            place = pl.multiple_of(at + end * stride, hr)
            edges[sep, :, pl.ds(place, hr)] = scaled[edge_row : edge_row + 1]

    rank_leaf_now = None
    for one in loads[:5]:
        one.wait()
    rank_leaf_now = rank_leaf[0]
    rank_middle_now = rank_middle[front // 2]
    weights[1] = 1.0 / spread(pivot_v[1], CW)
    for part, which in ((1, 1 - core), (0, core)):
        scaled, full = weighed(couple_m, which, weights[1], rank_middle_now)
        note(which * 6 * hr, hr, scaled)
        turned = full.T
        high = turned.astype(BF16)
        turned_high[part * hr : (part + 1) * hr, :] = high
        turned_low[part * hr : (part + 1) * hr, :] = (turned - high.astype(F32)).astype(BF16)

    loads[5].wait()

    def by_middle(part, right):
        block = slice(part * hr, (part + 1) * hr)
        return dot(turned_high[block, :], right) + dot(turned_low[block, :], right)

    pair_g_send[...] = by_middle(1, update_l[...])

    pl.semaphore_wait(barrier, n_sep + 2 + has_prev + has_next)

    def to_device(src, dst, send_sem, recv_sem, dom_at, sep_at):
        return pltpu.make_async_remote_copy(
            src, dst, send_sem, recv_sem, device_id=(dom_at, sep_at), device_id_type=MESH
        )

    pair_g = to_device(
        pair_g_send, pair_g_recv, pair_send_sem.at[0], pair_recv_sem.at[0], front, sibling
    )
    pair_g.start()
    g_own[...] = by_middle(0, update_l[...])

    for end, edge_row in ((0, rows - 1), (1, 0)):
        block = pl.ds(rows - TILE if end == 0 else 0, TILE)
        pick = TILE - 1 if end == 0 else 0
        row = update_l[block, :].astype(F32)[pick : pick + 1]
        edges[sep, :, (1 + end) * rank : (2 + end) * rank] = (
            row * weights[1, block, :][pick : pick + 1, :1]
        )

    for one in loads[6:8]:
        one.wait()
    live = (row_at < front_rows[0, 0]).astype(F32)
    weights[0] = live * (1.0 / spread(pivot_v[0], CW))
    for which in range(2):
        scaled, full = weighed(couple_l, which, weights[0], rank_leaf_now)
        note((8 + which) * hr, rank, scaled)
        turned = full.T
        high = turned.astype(BF16)
        turned_l[0, which * hr : (which + 1) * hr, :] = high
        turned_l[1, which * hr : (which + 1) * hr, :] = (turned - high.astype(F32)).astype(BF16)

    def edge_copy(k, sep_at, source, core_at):
        place = edges.at[source]
        if k not in (1, n_sep - 1):
            place = edges.at[source, :, pl.ds(pl.multiple_of(rank * core_at, rank), 6 * hr)]
        return to_device(
            place, place, edge_send_sem.at[sep_at], edge_recv_sem.at[source], front, sep_at
        )

    def edge_out(k):
        sep_at = lax.rem(sep + k, n_sep)
        return edge_copy(k, sep_at, sep, lax.rem(sep_at, 2))

    def edge_in(k):
        return edge_copy(n_sep - k, 0, lax.rem(sep + k, n_sep), core)

    near = (1, n_sep - 1)
    far = range(2, n_sep - 1)
    for k in near:
        edge_out(k).start()

    pair_g.wait_recv()
    summed = g_own[...] + pair_g_recv[...]
    g_own[...] = summed
    for part in range(PARTS):
        g_send[part] = summed[part * hp : (part + 1) * hp].astype(BF16)

    def g_copy(z_at, source, part):
        return to_device(
            g_send.at[part], g_recv.at[source, part], g_send_sem.at[z_at, part],
            g_recv_sem.at[source, part], front, 2 * z_at + core,
        )

    for k in far:
        edge_out(k).start()
    for part in range(PARTS):
        for k in range(1, n_z):
            g_copy(lax.rem(z + k, n_z), z, part).start()

    for one in loads[8:11]:
        one.wait()

    def tile_copies(way, sep_at):
        block = pl.ds(rows - TILE if way == 0 else 0, TILE)
        landing = pl.ds(rows + way * TILE, TILE)
        copies = [
            (pivot_v.at[2], pivot_edge.at[way], front),
            (top_v.at[block], top_edge.at[way], front),
            (update_m.at[group, block], update_m.at[group, landing], front),
            (update_m.at[group, block], update_m.at[group, landing], over),
        ]
        return [
            to_device(
                src, dst, tile_send_sem.at[way, n], tile_recv_sem.at[way, n], dom_at, sep_at
            )
            for n, (src, dst, dom_at) in enumerate(copies)
        ]

    to_next = tile_copies(0, sep + 1)
    to_prev = tile_copies(1, sep - 1)

    @pl.when(sep < n_sep - 1)
    def _():
        for copy in to_next:
            copy.start()

    @pl.when(sep > 0)
    def _():
        for copy in to_prev:
            copy.start()

    factor_copy = to_device(
        update_m.at[group, pl.ds(0, rows)], update_m.at[group, pl.ds(0, rows)],
        factor_send_sem.at[0], factor_recv_sem.at[0], over, sep,
    )
    factor_copy.start()
    weights[2] = 1.0 / spread(pivot_v[2], CW)

    for one in loads[11:]:
        one.wait()
    for k in near:
        edge_in(k).wait_recv()

    sixteen = lax.broadcasted_iota(jnp.int32, (TILE, hr), 0)
    before_at = jnp.maximum(sep - 1, 0)
    after_at = jnp.minimum(sep + 1, n_sep - 1)

    def two_rows(height_at, first, second):
        return jnp.where(height_at == 0, first, jnp.where(height_at == 1, second, 0.0)).astype(BF16)

    def neighbours(at, stride):
        before = edges[before_at, :, at : at + hr]
        after = edges[after_at, :, at + stride : at + stride + hr]
        return two_rows(
            sixteen, jnp.where(sep > 0, before, 0.0), jnp.where(sep < n_sep - 1, after, 0.0)
        )

    def end_rows(right, which, columns):
        first = right[0:TILE, columns].astype(F32)[0:1] * weights[which, 0:TILE, :][0:1, :1]
        last = (
            right[rows - TILE : rows, columns].astype(F32)[TILE - 1 :]
            * weights[which, rows - TILE : rows, :][TILE - 1 :, :1]
        )
        return two_rows(
            lax.broadcasted_iota(jnp.int32, (TILE, first.shape[1]), 0), first, last
        )

    edge_left[:, :hr] = neighbours(8 * hr, rank)
    edge_left[:, hr:] = neighbours(9 * hr, rank)

    def coef_copy(n):
        columns = pl.ds(n * quarter, quarter)
        return to_device(
            coef_l.at[pl.ds(0, rank), columns], coef_l.at[pl.ds(rank, rank), columns],
            coef_send_sem.at[n], coef_recv_sem.at[n], front, sibling,
        )

    for n in range(4):
        columns = slice(n * quarter, (n + 1) * quarter)
        coef_l[0:rank, columns] = (
            dot(turned_l[0], leaf_v[:, columns]) + dot(turned_l[1], leaf_v[:, columns])
            + dot_rows(edge_left[...], end_rows(leaf_v, 0, columns))
        ).astype(BF16)
        coef_copy(n).start()

    edge_left[:, :hr] = neighbours(0, hr)
    edge_left[:, hr:] = neighbours(6 * hr, hr)
    m_pair = to_device(m_send, m_recv, pair_send_sem.at[1], pair_recv_sem.at[1], front, sibling)
    for part, which, target in ((1, 1 - core, m_send), (0, core, m_own)):
        for n in range(2):
            columns = slice(n * quarter, (n + 1) * quarter)
            target[:, columns] = by_middle(part, middle_v[:, columns]) + dot_rows(
                edge_left[:, pl.ds(half_at(which), hr)], end_rows(middle_v, 1, columns)
            )
        if part == 1:
            m_pair.start()

    for k in far:
        edge_in(k).wait_recv()
    own_lanes = pl.multiple_of(core * 6 * hr, hr)
    for b in range(n_sep):
        if b < n_sep - 1:
            left = (
                edges[b, :, pl.ds(own_lanes, hr)], edges[b + 1, :, pl.ds(own_lanes + hr, hr)],
            )
            right = (
                edges[b + 1, :, 2 * rank : 3 * rank], edges[b, :, rank : 2 * rank],
            )
        else:
            left = (jnp.zeros((1, hr), F32),) * 2
            right = (jnp.zeros((1, rank), F32),) * 2
        for n in range(2):
            edge_right[2 * b + n : 2 * b + n + 1, :rank] = right[n]
            edge_right[2 * b + n : 2 * b + n + 1, rank:] = left[n]
    total = g_own[...] + dot_rows(
        edge_right[:, rank:].astype(BF16), edge_right[:, :rank].astype(BF16)
    )
    m_pair.wait_recv()
    m_own[...] += m_recv[...]
    for n in range(4):
        coef_copy(n).wait_recv()
    g_own[...] = total
    targets = (across, over, beyond)

    def p_copy(n, part, j):
        return to_device(
            p_send.at[n, part, j], p_recv.at[n, part, j], p_send_sem.at[n, part * n_top + j],
            p_recv_sem.at[n, part * n_top + j], targets[n], sep,
        )

    for part in range(PARTS):
        block = slice(part * hp, (part + 1) * hp)
        for k in range(1, n_z):
            source = lax.rem(z + k, n_z)
            g_copy(0, source, part).wait_recv()
            g_own[block, :] += g_recv[source, part].astype(F32)
        negated = -g_own[block, :]
        high = negated.astype(BF16)
        low = (negated - high.astype(F32)).astype(BF16)
        for n in range(2):
            lanes = slice(n * rank, (n + 1) * rank)
            g_twice[part, :hp, lanes] = high
            g_twice[part, hp:, lanes] = low

        def multiply(side_at, slot):
            at = pl.multiple_of(side_at * half, half)
            both = dot(g_twice[part], coef_l[:, pl.ds(at, half)])
            product[slot] = both[:hp] + both[hp:]

        def piece(slot, group_at, j):
            at = pl.multiple_of(group_at * quarter + j * CW, CW)
            return product[slot, :, pl.ds(at, CW)]

        multiply(1 - side, 0)
        for j in range(n_top):
            for n, group_at in ((2, 1 - group), (0, group)):
                p_send[n, part, j] = piece(0, group_at, j).astype(BF16)
                p_copy(n, part, j).start()
        multiply(side, 1)
        product[1] += m_own[block, :]
        for j in range(n_top):
            p_send[1, part, j] = piece(1, 1 - group, j).astype(BF16)
            p_copy(1, part, j).start()
            own[part * pieces + 2 * j] = piece(1, group, j)

    @pl.when(sep > 0)
    def _():
        for copy in to_next:
            copy.wait_recv()

    @pl.when(sep < n_sep - 1)
    def _():
        for copy in to_prev:
            copy.wait_recv()

    factor_copy.wait_recv()

    def right_copy(i):
        return to_device(
            right_send.at[i], right_recv.at[i], right_send_sem.at[i], right_recv_sem.at[i],
            front, sep + 2,
        )

    def left_copy(i):
        return to_device(
            left_send.at[i], left_recv.at[i], left_send_sem.at[i], left_recv_sem.at[i],
            front, sep - 2,
        )

    def place_of(i):
        at = lax.rem(i, 2)
        rest = lax.rem(i, pieces)
        start = pl.multiple_of(core * hr + lax.div(i, pieces) * hp, hp)
        return group + at - 2 * group * at, lax.div(rest, 2), pl.ds(start, hp)

    def final_copy(i):
        group_at, j, block = place_of(i)
        place = coef_m.at[group_at, j, block]
        return to_device(
            place, place, final_send_sem.at[i], final_recv_sem.at[i], front, sibling
        )

    def gather(i):
        part = lax.div(i, pieces)
        j = lax.div(lax.rem(i, pieces), 2)

        @pl.when(lax.rem(i, 2) == 0)
        def _():
            p_copy(0, part, j).wait_recv()
            own[i] += p_recv[0, part, j].astype(F32)

        @pl.when(lax.rem(i, 2) == 1)
        def _():
            p_copy(1, part, j).wait_recv()
            p_copy(2, part, j).wait_recv()
            own[i] = p_recv[1, part, j].astype(F32) + p_recv[2, part, j].astype(F32)

    def prefix(i):
        @pl.when(z > 0)
        def _():
            right_copy(i).wait_recv()

        @pl.when(z < n_z - 1)
        def _():
            right_send[i] = (own[i] + right_recv[i].astype(F32)).astype(BF16)
            right_copy(i).start()

    def suffix(i):
        @pl.when(z < n_z - 1)
        def _():
            left_copy(i).wait_recv()

        @pl.when(z > 0)
        def _():
            left_send[i] = (own[i] + left_recv[i].astype(F32)).astype(BF16)
            left_copy(i).start()

    def final(i):
        total = own[i] + right_recv[i].astype(F32) + left_recv[i].astype(F32)
        high = total.astype(BF16)
        low = (total - high.astype(F32)).astype(BF16)
        group_at, j, block = place_of(i)
        coef_m[group_at, j, block, :CW] = high
        coef_m[group_at, j, block, CW:] = low
        final_copy(i).start()

    def top(j):
        for part in range(PARTS):
            final_copy(part * pieces + 2 * j).wait_recv()
            final_copy(part * pieces + 2 * j + 1).wait_recv()
        at = pl.multiple_of(j * CW, CW)
        both = dot(update_m[0], coef_m[0, j]) + dot(update_m[1], coef_m[1, j])
        taken = both[:, :CW] + both[:, CW:]
        before = (
            top_edge[0, :, pl.ds(at, CW)].astype(F32)[TILE - 1 :]
            - taken[rows + TILE - 1 : rows + TILE]
        ) / pivot_edge[0, :, rows - 1 :]
        after = (
            top_edge[1, :, pl.ds(at, CW)].astype(F32)[:1] - taken[rows + TILE : rows + TILE + 1]
        ) / pivot_edge[1, :, :1]
        scaled = (top_v[:, pl.ds(at, CW)].astype(F32) - taken[:rows]) * weights[2]
        out[0, :, pl.ds(at, CW)] = scaled + weights[2] * shifted(scaled, before, after)

    last = jnp.maximum(z, n_z - 1 - z) * HOP
    steps = (n_z - 1) * HOP + items + LAND

    def step(t, carry):
        def on(at, count, body):
            @pl.when(jnp.logical_and(at >= 0, at < count))
            def _():
                body(at)

        on(t, items, gather)
        on(t - z * HOP, items, prefix)
        on(t - (n_z - 1 - z) * HOP, items, suffix)
        on(t - last, items, final)
        done = t - last - 1 - LAND - (items - pieces)

        @pl.when(jnp.logical_and(done >= 0, jnp.logical_and(done < pieces, lax.rem(done, 2) == 0)))
        def _():
            top(lax.div(done, 2))

        return carry

    lax.fori_loop(0, steps, step, 0)

    pair_g.wait_send()
    m_pair.wait_send()
    factor_copy.wait_send()
    for k in range(1, n_sep):
        edge_out(k).wait_send()
    for part in range(PARTS):
        for k in range(1, n_z):
            g_copy(lax.rem(z + k, n_z), z, part).wait_send()
    for n in range(4):
        coef_copy(n).wait_send()
    for n in range(3):
        for part in range(PARTS):
            for j in range(n_top):
                p_copy(n, part, j).wait_send()

    @pl.when(sep < n_sep - 1)
    def _():
        for copy in to_next:
            copy.wait_send()

    @pl.when(sep > 0)
    def _():
        for copy in to_prev:
            copy.wait_send()

    def drain(i, carry):
        @pl.when(z < n_z - 1)
        def _():
            right_copy(i).wait_send()

        @pl.when(z > 0)
        def _():
            left_copy(i).wait_send()

        final_copy(i).wait_send()
        return carry

    lax.fori_loop(0, items, drain, 0)


def shards(*operands):
    n_sep = lax.axis_size("sep")
    rows, width = operands[0].shape[1:]
    rank = operands[3].shape[2]
    half, quarter = width // 2, width // 4
    hr = rank // 2
    hp = hr // PARTS
    n_top = quarter // CW
    items = PARTS * 2 * n_top
    dma = pltpu.SemaphoreType.DMA
    hbm = pl.BlockSpec(memory_space=pltpu.HBM)
    vmem = pl.BlockSpec(memory_space=pltpu.VMEM)
    return pl.pallas_call(
        functools.partial(kernel, n_sep),
        out_shape=pltpu.VMEM((1, rows, quarter), F32),
        in_specs=[hbm] * 13,
        out_specs=vmem,
        scratch_shapes=[
            pltpu.SMEM(operands[10].shape, jnp.int32),
            pltpu.SMEM(operands[11].shape, jnp.int32),
            pltpu.SMEM(operands[12].shape, jnp.int32),
            pltpu.VMEM((3, 1, rows), F32),
            pltpu.VMEM((2, 1, rows), F32),
            pltpu.VMEM((rows, width), BF16),
            pltpu.VMEM((rows, half), BF16),
            pltpu.VMEM((rows, quarter), BF16),
            pltpu.VMEM((2, TILE, quarter), BF16),
            pltpu.VMEM((rows, rank), BF16),
            pltpu.VMEM((rows, rank), BF16),
            pltpu.VMEM((rows, rank), BF16),
            pltpu.VMEM((2, rows + 2 * TILE, rank), BF16),
            pltpu.VMEM((3, rows, CW), F32),
            pltpu.VMEM((2, rank, rows), BF16),
            pltpu.VMEM((rank, rows), BF16),
            pltpu.VMEM((rank, rows), BF16),
            pltpu.VMEM((n_sep, 1, 6 * rank), F32),
            pltpu.VMEM((TILE, rank), BF16),
            pltpu.VMEM((2 * n_sep, rank + hr), F32),
            pltpu.VMEM((hr, rank), F32),
            pltpu.VMEM((hr, rank), F32),
            pltpu.VMEM((hr, rank), F32),
            pltpu.VMEM((PARTS, hp, rank), BF16),
            pltpu.VMEM((n_sep // 2, PARTS, hp, rank), BF16),
            pltpu.VMEM((PARTS, 2 * hp, 2 * rank), BF16),
            pltpu.VMEM((2, hp, half), F32),
            pltpu.VMEM((2 * rank, width), BF16),
            pltpu.VMEM((hr, half), F32),
            pltpu.VMEM((hr, half), F32),
            pltpu.VMEM((hr, half), F32),
            pltpu.VMEM((3, PARTS, n_top, hp, CW), BF16),
            pltpu.VMEM((3, PARTS, n_top, hp, CW), BF16),
            pltpu.VMEM((items, hp, CW), F32),
            pltpu.VMEM((items, hp, CW), BF16),
            pltpu.VMEM((items, hp, CW), BF16),
            pltpu.VMEM((items, hp, CW), BF16),
            pltpu.VMEM((items, hp, CW), BF16),
            pltpu.VMEM((2, n_top, rank, 2 * CW), BF16),
            dma((13,)),
            dma((n_sep,)),
            dma((n_sep,)),
            dma((2, 4)),
            dma((2, 4)),
            dma((1,)),
            dma((1,)),
            dma((2,)),
            dma((2,)),
            dma((n_sep // 2, PARTS)),
            dma((n_sep // 2, PARTS)),
            dma((4,)),
            dma((4,)),
            dma((3, PARTS * n_top)),
            dma((3, PARTS * n_top)),
            dma((items,)),
            dma((items,)),
            dma((items,)),
            dma((items,)),
            dma((items,)),
            dma((items,)),
        ],
        compiler_params=pltpu.CompilerParams(
            collective_id=0, has_side_effects=True, vmem_limit_bytes=57543328
        ),
    )(*operands)


def solution(mesh):
    return jax.shard_map(
        shards,
        mesh=mesh,
        in_specs=(
            P("dom", "sep", None),
            P("dom", "sep", None),
            P("dom", "sep", None),
            P("dom", "sep", None),
            P("dom", "sep", None),
            P("dom", "sep", None),
            P("dom", "sep", None),
            P("dom", "sep"),
            P(None, "sep"),
            P(None, "sep"),
            P("dom", "sep"),
            P("dom"),
            P(),
        ),
        out_specs=P("dom", "sep", None),
        check_vma=False,
    )
```
